512 devices in a mesh: panel: 16 (over x_lo, y), inc: 32 (over x_hi, z, core).
Axes of the slice: x: 4 (x_hi: 2, x_lo: 2; x = x_hi * 2 + x_lo), y: 8, z: 8, core: 2. Of those that a mesh axis runs over, the one named last changes fastest.
Arguments:
- surface_field: bfloat16 [2, 512, 8192], P(None, 'inc', 'panel'), may hold values from -6 to 6
- near_block: bfloat16 [64, 128, 8, 2, 128], P('panel', 'inc'), may hold values from -0.125 to 0.125
- near_index: int32 [64, 8], P('panel'), may hold values from 0 to 63, as said below
- source_basis: bfloat16 [64, 2, 16, 128], P('panel'), may hold values from -0.375 to 0.375
- coupling: bfloat16 [64, 2, 16, 1024], P('panel'), may hold values from -0.1875 to 0.1875
- target_basis: bfloat16 [64, 2, 16, 128], P('panel'), may hold values from -1 to 1
- far_rank: int32 [64, 64], P('panel'), may hold values from 1 to 16, as said below
Outputs:
- applied_field: bfloat16 [2, 512, 8192], P(None, 'inc', 'panel')
The draws below stay inside these ranges and needn't reach their ends.
Inputs may be any that keep to these rules, and one draw needn't show every extreme that they name: `near_index`: each row names 8 distinct blocks within 4 blocks of its own block i around the closed order of blocks (index modulo 64); slot 0 names i, slot 1 names i - 4 and slot 2 names i + 4. `far_rank`: entries of pairs named in near_index are not used; every block i has rank 16 toward block i + 32.
All inputs are finite; a program needn't handle non-finite values.
Results may differ from the reference program's by a relative error of at most 0.0042.
Values may be sent and summed in bfloat16 or wider, within the bound.
A program may use at most 64 MiB of HBM per device.

```python
import jax
import jax.numpy as jnp
from jax import lax

BLK = 128
KN = 8
RMAX = 16
BPD = 4
NB = 64
PANELS = 8192
INC = 512


def draw_near_index(key, part):
    reach = BPD
    ahead = jnp.arange(1, reach, dtype=jnp.int32)
    candidates = jnp.concatenate([ahead, -ahead])
    keys = jax.random.split(key, NB)
    shuffled = jax.vmap(lambda single: jax.random.permutation(single, candidates))(keys)
    chosen = shuffled[:, :KN - 3]
    fixed = jnp.broadcast_to(jnp.array([0, -reach, reach], dtype=jnp.int32), (NB, 3))
    offsets = jnp.concatenate([fixed, chosen], axis=1)
    return (jnp.arange(NB, dtype=jnp.int32)[:, None] + offsets) % NB


def draw_far_rank(key, part):
    ranks = jax.random.randint(key, (NB, NB), 1, RMAX + 1, dtype=jnp.int32)
    rows = jnp.arange(NB, dtype=jnp.int32)[:, None]
    cols = jnp.arange(NB, dtype=jnp.int32)[None, :]
    partner = (rows + NB // 2) % NB
    return jnp.where(cols == partner, RMAX, ranks).astype(jnp.int32)


def block_scale(own_key, shape, cuts, smallest, high):
    def one(axis_at, shards_of):
        heights = jax.random.uniform(jax.random.fold_in(jax.random.fold_in(own_key, 6), axis_at), (shards_of,), jnp.float32, smallest / len(cuts), high / len(cuts))
        return jnp.repeat(jnp.exp(heights), shape[axis_at] // shards_of).reshape((-1,) + (1,) * (len(shape) - axis_at - 1))

    gain = one(*cuts[0])
    for cut in cuts[1:]:
        gain = gain * one(*cut)
    return gain


def scatter_about(stream_key, dims, spread, limit, shards=(), kind=jnp.bfloat16):
    values = jax.random.normal(stream_key, dims, jnp.float32) * spread
    if len(shards) > 0:
        values = block_scale(stream_key, dims, shards, -0.22, 0.18) * values
    return jnp.clip(values, min=-limit, max=limit).astype(kind)


def setup_inputs(seed: int = 0) -> dict:
    splits = jax.random.split(jax.random.key(seed), 8)
    return {
        "surface_field": scatter_about(splits[0], (2, INC, PANELS), 1.0, 6.0, ((1, 32), (2, 16))),
        "near_block": scatter_about(splits[1], (NB, BLK, KN, 2, BLK), (2 * KN * BLK) ** -0.5, 0.125, ((0, 16), (1, 32))),
        "near_index": draw_near_index(jax.random.fold_in(splits[7], 71), 0),
        "source_basis": scatter_about(splits[3], (NB, 2, RMAX, BLK), (2 * BLK) ** -0.5, 0.375, ((0, 16),)),
        "coupling": scatter_about(splits[4], (NB, 2, RMAX, NB * RMAX), (NB * RMAX) ** -0.5, 0.1875, ((0, 16),)),
        "target_basis": scatter_about(splits[5], (NB, 2, RMAX, BLK), (2 * RMAX) ** -0.5, 1.0, ((0, 16),)),
        "far_rank": draw_far_rank(jax.random.fold_in(splits[7], 71), 0),
    }


def reference(surface_field, near_block, near_index, source_basis, coupling, target_basis, far_rank):
    field_float = surface_field.astype(jnp.float32)
    field_blocks = field_float.reshape(2, INC, NB, BLK)
    vreal = source_basis[:, 0].astype(jnp.float32)
    vimag = source_basis[:, 1].astype(jnp.float32)
    part_a = jnp.einsum('jas,pmjs->pjam', vreal, field_blocks)
    part_b = jnp.einsum('jas,pmjs->pjam', vimag, field_blocks)
    compressed = jnp.stack([part_a[0] - part_b[1], part_a[1] + part_b[0]]).astype(jnp.bfloat16)
    compressed = compressed.reshape(2, NB * RMAX, INC).astype(jnp.float32)

    columns = jnp.arange(NB * RMAX, dtype=jnp.int32)
    within = columns % RMAX
    block_ids = jnp.arange(NB, dtype=jnp.int32)
    is_near = jnp.any(near_index[:, :, None] == block_ids[None, None, :], axis=1)
    rank_cols = jnp.repeat(far_rank, RMAX, axis=1)
    near_cols = jnp.repeat(is_near, RMAX, axis=1)
    rows_a = jnp.arange(RMAX, dtype=jnp.int32)
    keep = (rows_a[None, :, None] < rank_cols[:, None, :]) & (within[None, None, :] < rank_cols[:, None, :]) & jnp.logical_not(near_cols[:, None, :])
    masked = (coupling.astype(jnp.float32) * keep[:, None].astype(jnp.float32))
    part_a = jnp.einsum('iac,pcn->pian', masked[:, 0], compressed)
    part_b = jnp.einsum('iac,pcn->pian', masked[:, 1], compressed)
    mixed = jnp.stack([part_a[0] - part_b[1], part_a[1] + part_b[0]]).astype(jnp.bfloat16).astype(jnp.float32)
    ureal = target_basis[:, 0].astype(jnp.float32)
    uimag = target_basis[:, 1].astype(jnp.float32)
    part_a = jnp.einsum('iat,pian->pnit', ureal, mixed)
    part_b = jnp.einsum('iat,pian->pnit', uimag, mixed)
    far = jnp.stack([part_a[0] - part_b[1], part_a[1] + part_b[0]])

    def one_block(operands):
        coefs, picks = operands
        source = jnp.take(field_blocks, picks.astype(jnp.int32), axis=2)
        first_a = jnp.einsum('rks,pmks->pmr', coefs[:, :, 0].astype(jnp.float32), source)
        first_b = jnp.einsum('rks,pmks->pmr', coefs[:, :, 1].astype(jnp.float32), source)
        return jnp.stack([first_a[0] - first_b[1], first_a[1] + first_b[0]])

    near = lax.map(one_block, (near_block, near_index))
    near = jnp.transpose(near, (1, 2, 0, 3))
    result = field_blocks * 0.5 + near + far
    return result.reshape(2, INC, PANELS).astype(jnp.bfloat16)
```

```python
import functools

import jax
import jax.numpy as jnp
from jax import lax
from jax.experimental import pallas as pl
from jax.experimental.pallas import tpu as pltpu
from jax.sharding import PartitionSpec as P

MESH = pl.DeviceIdType.MESH
F32 = jnp.float32
BF16 = jnp.bfloat16
NT = (((1,), (1,)), ((), ()))


def dot_nt(a, b):
    return lax.dot_general(a, b, NT, preferred_element_type=F32)


def kernel(
    pn, zn,
    field, near, nidx_s, nidx_v, frank, sbasis, coup, tbasis,
    out,
    fbuf, nbuf, cbuf, ybuf, ysend, nraw, nf32, nv, fr, vb, cp, tb, mbuf, pmat, farbuf,
    lsem, fsend, frecv, nsend, nrecv, csend, crecv, ysnd, yrecv,
):
    p = lax.axis_index("panel")
    i = lax.axis_index("inc")
    xh = i // (2 * zn)
    z = (i // 2) % zn
    co = i % 2
    u = xh * 2 + co
    nb = pn * 4

    loads = [pltpu.make_async_copy(near, nraw, lsem.at[0])]
    for b in range(4):
        loads.append(
            pltpu.make_async_copy(field.at[:, :, pl.ds(b * 128, 128)], fbuf.at[4 + b, u], lsem.at[1 + b])
        )
    loads.append(pltpu.make_async_copy(sbasis, vb, lsem.at[5]))
    loads.append(pltpu.make_async_copy(coup, cp, lsem.at[6]))
    loads.append(pltpu.make_async_copy(tbasis, tb, lsem.at[7]))
    loads.append(pltpu.make_async_copy(nidx_v, nv, lsem.at[8]))
    loads.append(pltpu.make_async_copy(frank, fr, lsem.at[9]))
    for c in loads:
        c.start()

    def inc_of(xh_, z_, co_):
        return xh_ * (2 * zn) + z_ * 2 + co_

    npeers = [(p, inc_of(xh, (z + d) % zn, co)) for d in range(1, zn)]
    fpeers = []
    for dp in range(3):
        for du in range(4):
            if dp == 1 and du == 0:
                continue
            xo = (xh + du // 2) % 2
            cc = (co + du % 2) % 2
            fpeers.append((dp, du, ((p + dp - 1 + pn) % pn, inc_of(xo, z, cc))))
    cpeers = [((p + d) % pn, i) for d in range(1, pn)]

    barrier = pltpu.get_barrier_semaphore()
    everyone = npeers + [f[2] for f in fpeers] + cpeers
    for dev in everyone:
        pl.semaphore_signal(barrier, inc=1, device_id=dev, device_id_type=MESH)

    loads[0].wait()
    nf32[...] = nraw[...].astype(F32)
    for k in range(8):
        for c in range(2):
            rows = nf32[pl.ds(k * 2 + c, 16, stride=16), :]
            nbuf[c, z, :, k * 128 : (k + 1) * 128] = rows.astype(BF16)

    for c in loads[1:6]:
        c.wait()
    lane = lax.broadcasted_iota(jnp.int32, (32, 128), 1)
    low = lax.broadcasted_iota(jnp.int32, (16, 128), 1) < 64
    sbm = jnp.concatenate([vb[:, 0].reshape(64, 128), vb[:, 1].reshape(64, 128)], axis=0)
    own = fbuf[pl.ds(4, 4), u].reshape(128, 128)
    xall = dot_nt(own, sbm)
    xsel = jnp.zeros((32, 128), F32)
    for b in range(4):
        xsel = jnp.where((lane // 16) % 4 == b, xall[b * 32 : (b + 1) * 32], xsel)
    rolled = pltpu.roll(xsel[16:], 64, 1)
    cbuf[p] = (xsel[:16] + jnp.where(low, -rolled, rolled)).astype(BF16)

    pl.semaphore_wait(barrier, len(everyone))

    sends = []
    nsends = []
    for d in range(1, zn):
        nsends.append(
            pltpu.make_async_remote_copy(
                nbuf.at[:, z], nbuf.at[:, z], nsend.at[d], nrecv.at[d],
                device_id=npeers[d - 1], device_id_type=MESH,
            )
        )
    csends = []
    for d in range(1, pn):
        csends.append(
            pltpu.make_async_remote_copy(
                cbuf.at[p], cbuf.at[p], csend.at[d], crecv.at[d],
                device_id=cpeers[d - 1], device_id_type=MESH,
            )
        )
    fsends = []
    for dp, du, dev in fpeers:
        fsends.append(
            pltpu.make_async_remote_copy(
                fbuf.at[pl.ds(4, 4), u], fbuf.at[pl.ds((2 - dp) * 4, 4), u],
                fsend.at[dp * 4 + du], frecv.at[dp * 4 + du],
                device_id=dev, device_id_type=MESH,
            )
        )
    order = sorted(range(1, zn), key=lambda d: -min(d, zn - d))
    for d in order:
        nsends[d - 1].start()
    for c in csends:
        c.start()
    for c in fsends:
        c.start()

    for c in loads[6:]:
        c.wait()
    ids = lax.broadcasted_iota(jnp.int32, (4, nb), 1)
    is_near = nv[:, 0:1] == ids
    for k in range(1, 8):
        is_near = jnp.logical_or(is_near, nv[:, k : k + 1] == ids)
    rank = jnp.where(is_near, 0, fr[...]).astype(F32).astype(BF16)
    cols = nb * 16
    spread = (
        lax.broadcasted_iota(jnp.int32, (nb, cols), 1) // 16 == lax.broadcasted_iota(jnp.int32, (nb, cols), 0)
    ).astype(F32).astype(BF16)
    rank_cols = jnp.dot(rank, spread, preferred_element_type=F32)
    row_a = lax.broadcasted_iota(jnp.int32, (16, cols), 0).astype(F32)
    col_c = (lax.broadcasted_iota(jnp.int32, (16, cols), 1) % 16).astype(F32)
    most = jnp.maximum(row_a, col_c)
    for b in range(4):
        keep = most < jnp.broadcast_to(rank_cols[b : b + 1, :], (16, cols))
        for r in range(2):
            mbuf[r * 64 + b * 16 : r * 64 + b * 16 + 16, :] = jnp.where(
                keep, cp[b, r].astype(F32), 0.0
            ).astype(BF16)

    lanes_n = zn * 16
    width = 4 * lanes_n
    rr = lax.broadcasted_iota(jnp.int32, (width, width), 0)
    cc = lax.broadcasted_iota(jnp.int32, (width, width), 1)
    ru = rr // lanes_n
    rz = (rr // 16) % zn
    rb = (rr // 4) % 4
    rt = rr % 4
    target = rb * lanes_n + ((ru // 2) * (2 * zn) + rz * 2 + ru % 2) * 4 + rt
    pmat[...] = (cc == target).astype(F32).astype(BF16)

    for c in csends:
        c.wait_recv()
    re_tiles, im_tiles = [], []
    for q in range(pn // 2):
        even = cbuf[2 * q].astype(F32)
        odd = cbuf[2 * q + 1].astype(F32)
        re_tiles.append(jnp.where(low, even, pltpu.roll(odd, 64, 1)).astype(BF16))
        im_tiles.append(jnp.where(low, pltpu.roll(even, 64, 1), odd).astype(BF16))
    allc = jnp.concatenate(
        [jnp.concatenate(re_tiles, axis=1), jnp.concatenate(im_tiles, axis=1)], axis=0
    )
    omix = dot_nt(allc, mbuf[...])
    rolled = pltpu.roll(omix[16:], 64, 1)
    mixed = (omix[:16] + jnp.where(low, -rolled, rolled)).astype(BF16).astype(F32)
    lhs = jnp.concatenate([jnp.where(low, mixed, -mixed), pltpu.roll(mixed, 64, 1)], axis=0)
    lhs4 = jnp.concatenate(
        [jnp.where((lane // 16) % 4 == b, lhs, 0.0).astype(BF16) for b in range(4)], axis=0
    )
    tbm = jnp.concatenate([tb[:, 0].reshape(64, 128), tb[:, 1].reshape(64, 128)], axis=0)
    farbuf[...] = jnp.dot(lhs4, tbm, preferred_element_type=F32)

    for c in fsends:
        c.wait_recv()
    for c in nsends:
        c.wait_recv()
    amat = nbuf[...].reshape(2 * lanes_n, 8 * 128)
    lane2 = lax.broadcasted_iota(jnp.int32, (128, 2 * lanes_n), 1)
    ysum = jnp.zeros((128, 2 * lanes_n), F32)
    for b in range(4):
        parts = []
        for k in range(8):
            offset = jnp.minimum((nidx_s[b, k] - (p * 4 + b) + 4 + nb) % nb, 8)
            parts.append(fbuf[offset + b].reshape(128, 128))
        acc = dot_nt(jnp.concatenate(parts, axis=1), amat)
        ysum = jnp.where((lane2 // 4) % 4 == b, acc, ysum)
    for v in range(4):
        top = ysum[v * 32 : v * 32 + 16]
        bot = ysum[v * 32 + 16 : v * 32 + 32]
        ysend[v, 0:16] = top[:, :lanes_n] - bot[:, lanes_n:]
        ysend[v, 16:32] = top[:, lanes_n:] + bot[:, :lanes_n]
    ysends = []
    for du in range(1, 4):
        xo = (xh + du // 2) % 2
        cc_ = (co + du % 2) % 2
        ysends.append(
            pltpu.make_async_remote_copy(
                ysend.at[xo * 2 + cc_], ybuf.at[u], ysnd.at[du], yrecv.at[du],
                device_id=(p, inc_of(xo, z, cc_)), device_id_type=MESH,
            )
        )
    for c in ysends:
        c.start()
    ybuf[u] = ysend[u]
    for c in ysends:
        c.wait_recv()
    y = jnp.concatenate([ybuf[v] for v in range(4)], axis=1)
    hi = y.astype(BF16)
    lo = (y - hi.astype(F32)).astype(BF16)
    placed = jnp.dot(jnp.concatenate([hi, lo], axis=0), pmat[...], preferred_element_type=F32)
    placed = placed[:32] + placed[32:]
    for b in range(4):
        own_b = fbuf[4 + b, u].reshape(32, 128).astype(F32)
        res = own_b * 0.5 + placed[:, b * 128 : (b + 1) * 128] + farbuf[b * 32 : (b + 1) * 32]
        out[0, :, b * 128 : (b + 1) * 128] = res[:16].astype(BF16)
        out[1, :, b * 128 : (b + 1) * 128] = res[16:].astype(BF16)
    for c in nsends + csends + fsends + ysends:
        c.wait_send()


def solution(mesh):
    pn = mesh.shape["panel"]
    zn = mesh.shape["inc"] // 4
    nb = pn * 4
    width = 64 * zn

    def local(surface_field, near_block, near_index, source_basis, coupling, target_basis, far_rank):
        any_ = pl.BlockSpec(memory_space=pl.ANY)
        return pl.pallas_call(
            functools.partial(kernel, pn, zn),
            out_shape=jax.ShapeDtypeStruct(surface_field.shape, BF16),
            in_specs=[any_, any_, pl.BlockSpec(memory_space=pltpu.SMEM)] + [any_] * 5,
            out_specs=pl.BlockSpec(memory_space=pltpu.VMEM),
            scratch_shapes=[
                pltpu.VMEM((12, 4, 2, 16, 128), BF16),
                pltpu.VMEM((2, zn, 16, 1024), BF16),
                pltpu.VMEM((pn, 16, 128), BF16),
                pltpu.VMEM((4, 32, 16 * zn), F32),
                pltpu.VMEM((4, 32, 16 * zn), F32),
                pltpu.VMEM((256, 128), BF16),
                pltpu.VMEM((256, 128), F32),
                pltpu.VMEM((4, 8), jnp.int32),
                pltpu.VMEM((4, nb), jnp.int32),
                pltpu.VMEM((4, 2, 16, 128), BF16),
                pltpu.VMEM((4, 2, 16, nb * 16), BF16),
                pltpu.VMEM((4, 2, 16, 128), BF16),
                pltpu.VMEM((128, nb * 16), BF16),
                pltpu.VMEM((width, width), BF16),
                pltpu.VMEM((128, 128), F32),
                pltpu.SemaphoreType.DMA((10,)),
                pltpu.SemaphoreType.DMA((12,)),
                pltpu.SemaphoreType.DMA((12,)),
                pltpu.SemaphoreType.DMA((zn,)),
                pltpu.SemaphoreType.DMA((zn,)),
                pltpu.SemaphoreType.DMA((pn,)),
                pltpu.SemaphoreType.DMA((pn,)),
                pltpu.SemaphoreType.DMA((4,)),
                pltpu.SemaphoreType.DMA((4,)),
            ],
            compiler_params=pltpu.CompilerParams(collective_id=0, has_side_effects=True),
        )(
            surface_field, near_block.reshape(256, 128), near_index, near_index, far_rank,
            source_basis, coupling, target_basis,
        )

    return jax.shard_map(
        local,
        mesh=mesh,
        in_specs=(
            P(None, "inc", "panel"),
            P("panel", "inc", None, None, None),
            P("panel", None),
            P("panel", None, None, None),
            P("panel", None, None, None),
            P("panel", None, None, None),
            P("panel", None),
        ),
        out_specs=P(None, "inc", "panel"),
        check_vma=False,
    )
```

```python
import functools

import jax
import jax.numpy as jnp
from jax import lax
from jax.experimental import pallas as pl
from jax.experimental.pallas import tpu as pltpu
from jax.sharding import PartitionSpec as P

MESH = pl.DeviceIdType.MESH
F32 = jnp.float32
BF16 = jnp.bfloat16
NT = (((1,), (1,)), ((), ()))


def dot_nt(a, b):
    return lax.dot_general(a, b, NT, preferred_element_type=F32)


def kernel(
    pn, zn,
    field, near, nidx_s, nidx_v, frank, sbasis, coup, tbasis,
    out,
    fbuf, nbuf, cbuf, ybuf, ysend, nraw, nf32, nv, fr, vb, cp, tb, mbuf, pmat, farbuf,
    lsem, fsend, frecv, nsend, nrecv, rsend, csend, crecv, heard, ysnd, yrecv, ready,
):
    p = lax.axis_index("panel")
    i = lax.axis_index("inc")
    xh = i // (2 * zn)
    z = (i // 2) % zn
    co = i % 2
    u = xh * 2 + co
    nb = pn * 4

    loads = [pltpu.make_async_copy(near, nraw, lsem.at[0])]
    for b in range(4):
        loads.append(
            pltpu.make_async_copy(field.at[:, :, pl.ds(b * 128, 128)], fbuf.at[4 + b, u], lsem.at[1 + b])
        )
    loads.append(pltpu.make_async_copy(sbasis, vb, lsem.at[5]))
    loads.append(pltpu.make_async_copy(coup, cp, lsem.at[6]))
    loads.append(pltpu.make_async_copy(tbasis, tb, lsem.at[7]))
    loads.append(pltpu.make_async_copy(nidx_v, nv, lsem.at[8]))
    loads.append(pltpu.make_async_copy(frank, fr, lsem.at[9]))
    for c in loads:
        c.start()

    def inc_of(xh_, z_, co_):
        return xh_ * (2 * zn) + z_ * 2 + co_

    npeers = [(p, inc_of(xh, other, co)) for other in range(zn)]
    below = (p, inc_of(xh, (z + zn - 1) % zn, co))
    reach = zn // 2 - 1

    def close(a, b):
        return min((a - b) % zn, (b - a) % zn) <= reach

    yn = pn // 2
    first = (p // yn) * yn
    y = p % yn
    y_next = (first + (y + 1) % yn, i)
    y_prev = (first + (y + yn - 1) % yn, i)
    column = ((p + yn) % pn, i)
    fpeers = []
    for dp in range(3):
        for du in range(4):
            if dp == 1 and du == 0:
                continue
            xo = (xh + du // 2) % 2
            cc = (co + du % 2) % 2
            fpeers.append((dp, du, ((p + dp - 1 + pn) % pn, inc_of(xo, z, cc))))

    barrier = pltpu.get_barrier_semaphore()
    plane = [f[2] for f in fpeers] + [y_next, y_prev, column]

    for at in range(zn - 1):

        @pl.when(z == at)
        def _():
            for other in range(at + 1, zn):
                if close(at, other):
                    pl.semaphore_signal(barrier, inc=1, device_id=npeers[other], device_id_type=MESH)

    for dev in plane:
        pl.semaphore_signal(barrier, inc=1, device_id=dev, device_id_type=MESH)

    loads[0].wait()
    nf32[...] = nraw[...].astype(F32)
    for k in range(8):
        for c in range(2):
            rows = nf32[pl.ds(k * 2 + c, 16, stride=16), :]
            nbuf[c, z, :, k * 128 : (k + 1) * 128] = rows.astype(BF16)

    for c in loads[1:6]:
        c.wait()
    lane = lax.broadcasted_iota(jnp.int32, (32, 128), 1)
    low = lax.broadcasted_iota(jnp.int32, (16, 128), 1) < 64
    sbm = jnp.concatenate([vb[:, 0].reshape(64, 128), vb[:, 1].reshape(64, 128)], axis=0)
    own = fbuf[pl.ds(4, 4), u].reshape(128, 128)
    xall = dot_nt(own, sbm)
    xsel = jnp.zeros((32, 128), F32)
    for b in range(4):
        xsel = jnp.where((lane // 16) % 4 == b, xall[b * 32 : (b + 1) * 32], xsel)
    rolled = pltpu.roll(xsel[16:], 64, 1)
    cbuf[p] = (xsel[:16] + jnp.where(low, -rolled, rolled)).astype(BF16)

    earlier = 0
    for at in range(1, zn):
        earlier = earlier + jnp.where(z == at, sum(close(at, other) for other in range(at)), 0)
    pl.semaphore_wait(barrier, len(plane) + earlier)

    def near_copy(other, at):
        return pltpu.make_async_remote_copy(
            nbuf.at[:, at], nbuf.at[:, at], nsend.at[other], nrecv.at[at],
            device_id=npeers[other], device_id_type=MESH,
        )

    def near_arrived(chunk):
        pltpu.make_async_remote_copy(
            nbuf.at[:, chunk], nbuf.at[:, chunk], nsend.at[chunk], nrecv.at[chunk],
            device_id=npeers[chunk], device_id_type=MESH,
        ).wait_recv()

    def relay(at):
        chunk = (at + reach) % zn
        return pltpu.make_async_remote_copy(
            nbuf.at[:, chunk], nbuf.at[:, chunk], rsend, nrecv.at[chunk],
            device_id=below, device_id_type=MESH,
        )

    csends = [
        pltpu.make_async_remote_copy(
            cbuf.at[p], cbuf.at[p], csend.at[d], crecv.at[d], device_id=((p + d) % pn, i), device_id_type=MESH
        )
        for d in range(1, pn)
    ]
    hops = yn // 2 - 1

    def c_step(step):
        if 0 < step <= hops:
            pl.semaphore_wait(heard.at[2 * step - 2], 1)
            pl.semaphore_wait(heard.at[2 * step - 1], 1)
        if step < hops:
            pl.semaphore_signal(heard.at[2 * step], inc=1, device_id=y_next, device_id_type=MESH)
            pl.semaphore_signal(heard.at[2 * step + 1], inc=1, device_id=y_prev, device_id_type=MESH)
        elif step == hops:
            pl.semaphore_signal(heard.at[2 * hops], inc=1, device_id=column, device_id_type=MESH)
        else:
            pl.semaphore_wait(heard.at[2 * hops], 1)
            for c in csends:
                c.start()

    def run(ops, at):
        for op in ops:
            kind, step = op[0], int(op[1])
            if kind == "C":
                c_step(step)
            elif kind == "S":
                pl.semaphore_wait(ready.at[step], 1)
                near_copy(step, at).start()
            else:
                near_arrived((at + reach) % zn)
                relay(at).start()

    for at in range(1, zn):

        @pl.when(z == at)
        def _():
            for other in range(at):
                if close(at, other):
                    near_copy(other, at).start()
                    pl.semaphore_signal(ready.at[at], inc=1, device_id=npeers[other], device_id_type=MESH)

    c_step(0)
    fsends = []
    for dp, du, dev in fpeers:
        fsends.append(
            pltpu.make_async_remote_copy(
                fbuf.at[pl.ds(4, 4), u], fbuf.at[pl.ds((2 - dp) * 4, 4), u],
                fsend.at[dp * 4 + du], frecv.at[dp * 4 + du],
                device_id=dev, device_id_type=MESH,
            )
        )
    for c in fsends:
        c.start()

    for c in loads[6:]:
        c.wait()
    ids = lax.broadcasted_iota(jnp.int32, (4, nb), 1)
    is_near = nv[:, 0:1] == ids
    for k in range(1, 8):
        is_near = jnp.logical_or(is_near, nv[:, k : k + 1] == ids)
    rank = jnp.where(is_near, 0, fr[...]).astype(F32).astype(BF16)
    cols = nb * 16
    spread = (
        lax.broadcasted_iota(jnp.int32, (nb, cols), 1) // 16 == lax.broadcasted_iota(jnp.int32, (nb, cols), 0)
    ).astype(F32).astype(BF16)
    rank_cols = jnp.dot(rank, spread, preferred_element_type=F32)
    row_a = lax.broadcasted_iota(jnp.int32, (16, cols), 0).astype(F32)
    col_c = (lax.broadcasted_iota(jnp.int32, (16, cols), 1) % 16).astype(F32)
    most = jnp.maximum(row_a, col_c)
    for b in range(4):
        keep = most < jnp.broadcast_to(rank_cols[b : b + 1, :], (16, cols))
        for r in range(2):
            mbuf[r * 64 + b * 16 : r * 64 + b * 16 + 16, :] = jnp.where(
                keep, cp[b, r].astype(F32), 0.0
            ).astype(BF16)

    lanes_n = zn * 16
    width = 4 * lanes_n
    rr = lax.broadcasted_iota(jnp.int32, (width, width), 0)
    cc = lax.broadcasted_iota(jnp.int32, (width, width), 1)
    group = width // 2
    ru = (rr % group) // 64
    rz = (z + (rr // group) * 4 + (rr % 64) // 16) % zn
    rb = (rr // 4) % 4
    rt = rr % 4
    target = rb * lanes_n + ((ru // 2) * (2 * zn) + rz * 2 + ru % 2) * 4 + rt
    pmat[...] = (cc == target).astype(F32).astype(BF16)

    early = [
        ("C1", "C2", "S1", "C3", "C4", "S2", "S3", "S5", "S6", "S7", "F0"),
        ("C1", "C2", "S2", "C3", "C4", "S3", "S4", "F0", "S6", "S7"),
        ("C1", "C2", "S3", "C3", "C4", "S4", "S5", "F0", "S7"),
        ("C1", "C2", "S4", "C3", "C4", "S5", "S6", "F0"),
        ("C1", "C2", "S5", "C3", "C4", "S6", "S7", "F0"),
        ("C1", "C2", "S6", "C3", "C4", "S7", "F0"),
        ("C1", "C2", "S7", "C3", "C4", "F0"),
        ("C1", "C2", "C3", "C4", "F0"),
    ]
    for at in range(zn):

        @pl.when(z == at)
        def _():
            run(early[at], at)

    for c in csends:
        c.wait_recv()

    re_tiles, im_tiles = [], []
    for q in range(pn // 2):
        even = cbuf[2 * q].astype(F32)
        odd = cbuf[2 * q + 1].astype(F32)
        re_tiles.append(jnp.where(low, even, pltpu.roll(odd, 64, 1)).astype(BF16))
        im_tiles.append(jnp.where(low, pltpu.roll(even, 64, 1), odd).astype(BF16))
    allc = jnp.concatenate(
        [jnp.concatenate(re_tiles, axis=1), jnp.concatenate(im_tiles, axis=1)], axis=0
    )
    omix = dot_nt(allc, mbuf[...])
    rolled = pltpu.roll(omix[16:], 64, 1)
    mixed = (omix[:16] + jnp.where(low, -rolled, rolled)).astype(BF16).astype(F32)
    lhs = jnp.concatenate([jnp.where(low, mixed, -mixed), pltpu.roll(mixed, 64, 1)], axis=0)
    lhs4 = jnp.concatenate(
        [jnp.where((lane // 16) % 4 == b, lhs, 0.0).astype(BF16) for b in range(4)], axis=0
    )
    tbm = jnp.concatenate([tb[:, 0].reshape(64, 128), tb[:, 1].reshape(64, 128)], axis=0)
    farbuf[...] = jnp.dot(lhs4, tbm, preferred_element_type=F32)

    for c in fsends:
        c.wait_recv()
    picks = []
    for b in range(4):
        picks.append(
            [jnp.minimum((nidx_s[b, k] - (p * 4 + b) + 4 + nb) % nb, 8) + b for k in range(8)]
        )
    lane2 = lax.broadcasted_iota(jnp.int32, (128, 128), 1)
    ysends = []
    for g in range(2):
        for at in range(zn):

            @pl.when(z == at)
            def _():
                for place in range(g * 4, g * 4 + 4):
                    chunk = (at + place) % zn
                    if place not in (0, reach):
                        near_arrived(chunk)

        amat = jnp.concatenate(
            [nbuf[c, (z + g * 4 + place) % zn] for c in range(2) for place in range(4)], axis=0
        )
        ysum = jnp.zeros((128, 128), F32)
        for b in range(4):
            rows_b = jnp.concatenate([fbuf[j].reshape(128, 128) for j in picks[b]], axis=1)
            ysum = jnp.where((lane2 // 4) % 4 == b, dot_nt(rows_b, amat), ysum)
        for v in range(4):
            turned = pltpu.roll(ysum[v * 32 + 16 : v * 32 + 32], 64, 1)
            ysend[g, v] = ysum[v * 32 : v * 32 + 16] + jnp.where(low, -turned, turned)
        for du in (3, 2, 1):
            xo = (xh + du // 2) % 2
            cc_ = (co + du % 2) % 2
            copy = pltpu.make_async_remote_copy(
                ysend.at[g, xo * 2 + cc_], ybuf.at[g, u], ysnd.at[g, du], yrecv.at[g, du],
                device_id=(p, inc_of(xo, z, cc_)), device_id_type=MESH,
            )
            copy.start()
            ysends.append(copy)
        ybuf[g, u] = ysend[g, u]
    for c in ysends:
        c.wait_recv()
    res_re, res_im = [], []
    for g in range(2):
        for v in (0, 2):
            even, odd = ybuf[g, v], ybuf[g, v + 1]
            res_re.append(jnp.where(low, even, pltpu.roll(odd, 64, 1)))
            res_im.append(jnp.where(low, pltpu.roll(even, 64, 1), odd))
    result = jnp.concatenate(
        [jnp.concatenate(res_re, axis=1), jnp.concatenate(res_im, axis=1)], axis=0
    )
    hi = result.astype(BF16)
    lo = (result - hi.astype(F32)).astype(BF16)
    placed = jnp.dot(jnp.concatenate([hi, lo], axis=0), pmat[...], preferred_element_type=F32)
    placed = placed[:32] + placed[32:]
    for b in range(4):
        own_b = fbuf[4 + b, u].reshape(32, 128).astype(F32)
        res = own_b * 0.5 + placed[:, b * 128 : (b + 1) * 128] + farbuf[b * 32 : (b + 1) * 32]
        out[0, :, b * 128 : (b + 1) * 128] = res[:16].astype(BF16)
        out[1, :, b * 128 : (b + 1) * 128] = res[16:].astype(BF16)
    for c in fsends + ysends:
        c.wait_send()
    for c in csends:
        c.wait_send()
    for at in range(zn):

        @pl.when(z == at)
        def _():
            for other in range(zn):
                if other != at and close(at, other):
                    near_copy(other, at).wait_send()
            relay(at).wait_send()


def solution(mesh):
    pn = mesh.shape["panel"]
    zn = mesh.shape["inc"] // 4
    nb = pn * 4
    width = 64 * zn

    def local(surface_field, near_block, near_index, source_basis, coupling, target_basis, far_rank):
        any_ = pl.BlockSpec(memory_space=pl.ANY)
        return pl.pallas_call(
            functools.partial(kernel, pn, zn),
            out_shape=jax.ShapeDtypeStruct(surface_field.shape, BF16),
            in_specs=[any_, any_, pl.BlockSpec(memory_space=pltpu.SMEM)] + [any_] * 5,
            out_specs=pl.BlockSpec(memory_space=pltpu.VMEM),
            scratch_shapes=[
                pltpu.VMEM((12, 4, 2, 16, 128), BF16),
                pltpu.VMEM((2, zn, 16, 1024), BF16),
                pltpu.VMEM((pn, 16, 128), BF16),
                pltpu.VMEM((2, 4, 16, 128), F32),
                pltpu.VMEM((2, 4, 16, 128), F32),
                pltpu.VMEM((256, 128), BF16),
                pltpu.VMEM((256, 128), F32),
                pltpu.VMEM((4, 8), jnp.int32),
                pltpu.VMEM((4, nb), jnp.int32),
                pltpu.VMEM((4, 2, 16, 128), BF16),
                pltpu.VMEM((4, 2, 16, nb * 16), BF16),
                pltpu.VMEM((4, 2, 16, 128), BF16),
                pltpu.VMEM((128, nb * 16), BF16),
                pltpu.VMEM((width, width), BF16),
                pltpu.VMEM((128, 128), F32),
                pltpu.SemaphoreType.DMA((10,)),
                pltpu.SemaphoreType.DMA((12,)),
                pltpu.SemaphoreType.DMA((12,)),
                pltpu.SemaphoreType.DMA((zn,)),
                pltpu.SemaphoreType.DMA((zn,)),
                pltpu.SemaphoreType.DMA,
                pltpu.SemaphoreType.DMA((pn,)),
                pltpu.SemaphoreType.DMA((pn,)),
                pltpu.SemaphoreType.REGULAR((8,)),
                pltpu.SemaphoreType.DMA((2, 4)),
                pltpu.SemaphoreType.DMA((2, 4)),
                pltpu.SemaphoreType.REGULAR((zn,)),
            ],
            compiler_params=pltpu.CompilerParams(collective_id=0, has_side_effects=True),
        )(
            surface_field, near_block.reshape(256, 128), near_index, near_index, far_rank,
            source_basis, coupling, target_basis,
        )

    return jax.shard_map(
        local,
        mesh=mesh,
        in_specs=(
            P(None, "inc", "panel"),
            P("panel", "inc", None, None, None),
            P("panel", None),
            P("panel", None, None, None),
            P("panel", None, None, None),
            P("panel", None, None, None),
            P("panel", None),
        ),
        out_specs=P(None, "inc", "panel"),
        check_vma=False,
    )
```

```python
import functools

import jax
import jax.numpy as jnp
from jax import lax
from jax.experimental import pallas as pl
from jax.experimental.pallas import tpu as pltpu
from jax.sharding import PartitionSpec as P

MESH = pl.DeviceIdType.MESH
F32 = jnp.float32
BF16 = jnp.bfloat16
NT = (((1,), (1,)), ((), ()))


def dot_nt(a, b):
    return lax.dot_general(a, b, NT, preferred_element_type=F32)


def kernel(
    pn, zn,
    field, near, nidx_s, nidx_v, frank, sbasis, coup, tbasis,
    out,
    fbuf, nbuf, cbuf, ybuf, ysend, nraw, nf32, nv, fr, vb, cp, tb, mbuf, pmat, farbuf,
    lsem, fsend, frecv, nsend, nrecv, rsend, csend, crecv, heard, met, ysnd, yrecv, ready,
):
    p = lax.axis_index("panel")
    i = lax.axis_index("inc")
    xh = i // (2 * zn)
    z = (i // 2) % zn
    co = i % 2
    u = xh * 2 + co
    nb = pn * 4

    loads = [pltpu.make_async_copy(near, nraw, lsem.at[0])]
    for b in range(4):
        loads.append(
            pltpu.make_async_copy(field.at[:, :, pl.ds(b * 128, 128)], fbuf.at[4 + b, u], lsem.at[1 + b])
        )
    loads.append(pltpu.make_async_copy(sbasis, vb, lsem.at[5]))
    loads.append(pltpu.make_async_copy(coup, cp, lsem.at[6]))
    loads.append(pltpu.make_async_copy(tbasis, tb, lsem.at[7]))
    loads.append(pltpu.make_async_copy(nidx_v, nv, lsem.at[8]))
    loads.append(pltpu.make_async_copy(frank, fr, lsem.at[9]))
    for c in loads:
        c.start()

    def inc_of(xh_, z_, co_):
        return xh_ * (2 * zn) + z_ * 2 + co_

    npeers = [(p, inc_of(xh, other, co)) for other in range(zn)]
    below = (p, inc_of(xh, (z + zn - 1) % zn, co))
    reach = zn // 2 - 1

    def close(a, b):
        return min((a - b) % zn, (b - a) % zn) <= reach

    yn = pn // 2
    first = (p // yn) * yn
    y = p % yn
    y_next = (first + (y + 1) % yn, i)
    y_prev = (first + (y + yn - 1) % yn, i)
    column = ((p + yn) % pn, i)
    fpeers = []
    for dp in range(3):
        for du in range(4):
            if dp == 1 and du == 0:
                continue
            xo = (xh + du // 2) % 2
            cc = (co + du % 2) % 2
            fpeers.append((dp, du, ((p + dp - 1 + pn) % pn, inc_of(xo, z, cc))))

    barrier = pltpu.get_barrier_semaphore()
    high = (p, inc_of((xh + 1) % 2, z, co))
    p_next, p_prev = ((p + 1) % pn, i), ((p + pn - 1) % pn, i)
    plane = [(p, inc_of(xh, z, (co + 1) % 2)), high, p_next, p_prev, y_next, y_prev, column]

    for at in range(zn - 1):

        @pl.when(z == at)
        def _():
            for other in range(at + 1, zn):
                if close(at, other):
                    pl.semaphore_signal(barrier, inc=1, device_id=npeers[other], device_id_type=MESH)

    for dev in plane:
        pl.semaphore_signal(barrier, inc=1, device_id=dev, device_id_type=MESH)

    loads[0].wait()
    nf32[...] = nraw[...].astype(F32)
    for k in range(8):
        for c in range(2):
            rows = nf32[pl.ds(k * 2 + c, 16, stride=16), :]
            nbuf[c, z, :, k * 128 : (k + 1) * 128] = rows.astype(BF16)

    earlier = 0
    for at in range(1, zn):
        earlier = earlier + jnp.where(z == at, sum(close(at, other) for other in range(at)), 0)
    pl.semaphore_wait(barrier, len(plane) + earlier)

    def near_copy(other, at):
        return pltpu.make_async_remote_copy(
            nbuf.at[:, at], nbuf.at[:, at], nsend.at[other], nrecv.at[at],
            device_id=npeers[other], device_id_type=MESH,
        )

    def near_arrived(chunk):
        pltpu.make_async_remote_copy(
            nbuf.at[:, chunk], nbuf.at[:, chunk], nsend.at[chunk], nrecv.at[chunk],
            device_id=npeers[chunk], device_id_type=MESH,
        ).wait_recv()

    def relay(at):
        chunk = (at + reach) % zn
        return pltpu.make_async_remote_copy(
            nbuf.at[:, chunk], nbuf.at[:, chunk], rsend, nrecv.at[chunk],
            device_id=below, device_id_type=MESH,
        )

    csends = [
        pltpu.make_async_remote_copy(
            cbuf.at[p], cbuf.at[p], csend.at[d], crecv.at[d], device_id=((p + d) % pn, i), device_id_type=MESH
        )
        for d in range(1, pn)
    ]
    hops = yn // 2 - 1

    def c_step(step):
        if 0 < step <= hops:
            pl.semaphore_wait(heard.at[2 * step - 2], 1)
            pl.semaphore_wait(heard.at[2 * step - 1], 1)
        if step < hops:
            pl.semaphore_signal(heard.at[2 * step], inc=1, device_id=y_next, device_id_type=MESH)
            pl.semaphore_signal(heard.at[2 * step + 1], inc=1, device_id=y_prev, device_id_type=MESH)
        elif step == hops:
            pl.semaphore_signal(heard.at[2 * hops], inc=1, device_id=column, device_id_type=MESH)
        else:
            pl.semaphore_wait(heard.at[2 * hops], 1)
            for c in csends:
                c.start()

    def run(ops, at):
        for op in ops:
            kind, step = op[0], int(op[1])
            if kind == "C":
                c_step(step)
            elif kind == "S":
                pl.semaphore_wait(ready.at[step], 1)
                near_copy(step, at).start()
            else:
                near_arrived((at + reach) % zn)
                relay(at).start()

    for at in range(1, zn):

        @pl.when(z == at)
        def _():
            lower = [other for other in range(at) if close(at, other)]
            for other in lower:
                pl.semaphore_signal(ready.at[at], inc=1, device_id=npeers[other], device_id_type=MESH)
            for other in lower:
                near_copy(other, at).start()

    pl.semaphore_signal(met.at[0], inc=1, device_id=high, device_id_type=MESH)
    c_step(0)
    fsends = []
    for dp, du, dev in fpeers:
        fsends.append(
            pltpu.make_async_remote_copy(
                fbuf.at[pl.ds(4, 4), u], fbuf.at[pl.ds((2 - dp) * 4, 4), u],
                fsend.at[dp * 4 + du], frecv.at[dp * 4 + du],
                device_id=dev, device_id_type=MESH,
            )
        )
    for c in loads[1:5]:
        c.wait()
    pl.semaphore_wait(met.at[0], 1)
    pl.semaphore_signal(met.at[1], inc=1, device_id=p_next, device_id_type=MESH)
    pl.semaphore_signal(met.at[2], inc=1, device_id=p_prev, device_id_type=MESH)

    loads[5].wait()
    lane = lax.broadcasted_iota(jnp.int32, (32, 128), 1)
    low = lax.broadcasted_iota(jnp.int32, (16, 128), 1) < 64
    sbm = jnp.concatenate([vb[:, 0].reshape(64, 128), vb[:, 1].reshape(64, 128)], axis=0)
    own = fbuf[pl.ds(4, 4), u].reshape(128, 128)
    xall = dot_nt(own, sbm)
    xsel = jnp.zeros((32, 128), F32)
    for b in range(4):
        xsel = jnp.where((lane // 16) % 4 == b, xall[b * 32 : (b + 1) * 32], xsel)
    rolled = pltpu.roll(xsel[16:], 64, 1)
    cbuf[p] = (xsel[:16] + jnp.where(low, -rolled, rolled)).astype(BF16)

    pl.semaphore_wait(met.at[1], 1)
    pl.semaphore_wait(met.at[2], 1)
    for c in fsends:
        c.start()

    for c in loads[6:]:
        c.wait()
    ids = lax.broadcasted_iota(jnp.int32, (4, nb), 1)
    is_near = nv[:, 0:1] == ids
    for k in range(1, 8):
        is_near = jnp.logical_or(is_near, nv[:, k : k + 1] == ids)
    rank = jnp.where(is_near, 0, fr[...]).astype(F32).astype(BF16)
    cols = nb * 16
    spread = (
        lax.broadcasted_iota(jnp.int32, (nb, cols), 1) // 16 == lax.broadcasted_iota(jnp.int32, (nb, cols), 0)
    ).astype(F32).astype(BF16)
    rank_cols = jnp.dot(rank, spread, preferred_element_type=F32)
    row_a = lax.broadcasted_iota(jnp.int32, (16, cols), 0).astype(F32)
    col_c = (lax.broadcasted_iota(jnp.int32, (16, cols), 1) % 16).astype(F32)
    most = jnp.maximum(row_a, col_c)
    for b in range(4):
        keep = most < jnp.broadcast_to(rank_cols[b : b + 1, :], (16, cols))
        for r in range(2):
            mbuf[r * 64 + b * 16 : r * 64 + b * 16 + 16, :] = jnp.where(
                keep, cp[b, r].astype(F32), 0.0
            ).astype(BF16)

    lanes_n = zn * 16
    width = 4 * lanes_n
    rr = lax.broadcasted_iota(jnp.int32, (width, width), 0)
    cc = lax.broadcasted_iota(jnp.int32, (width, width), 1)
    group = width // 2
    ru = (rr % group) // 64
    rz = (z + (rr // group) * 4 + (rr % 64) // 16) % zn
    rb = (rr // 4) % 4
    rt = rr % 4
    target = rb * lanes_n + ((ru // 2) * (2 * zn) + rz * 2 + ru % 2) * 4 + rt
    pmat[...] = (cc == target).astype(F32).astype(BF16)

    early = [
        ("C1", "C2", "S1", "C3", "C4", "S2", "S3", "S5", "S6", "S7", "F0"),
        ("C1", "C2", "S2", "C3", "C4", "S3", "S4", "F0", "S6", "S7"),
        ("C1", "C2", "S3", "C3", "C4", "S4", "S5", "F0", "S7"),
        ("C1", "C2", "S4", "C3", "C4", "S5", "S6", "F0"),
        ("C1", "C2", "S5", "C3", "C4", "S6", "S7", "F0"),
        ("C1", "C2", "S6", "C3", "C4", "S7", "F0"),
        ("C1", "C2", "S7", "C3", "C4", "F0"),
        ("C1", "C2", "C3", "C4", "F0"),
    ]
    for at in range(zn):

        @pl.when(z == at)
        def _():
            run(early[at], at)

    for c in csends:
        c.wait_recv()

    re_tiles, im_tiles = [], []
    for q in range(pn // 2):
        even = cbuf[2 * q].astype(F32)
        odd = cbuf[2 * q + 1].astype(F32)
        re_tiles.append(jnp.where(low, even, pltpu.roll(odd, 64, 1)).astype(BF16))
        im_tiles.append(jnp.where(low, pltpu.roll(even, 64, 1), odd).astype(BF16))
    allc = jnp.concatenate(
        [jnp.concatenate(re_tiles, axis=1), jnp.concatenate(im_tiles, axis=1)], axis=0
    )
    omix = dot_nt(allc, mbuf[...])
    rolled = pltpu.roll(omix[16:], 64, 1)
    mixed = (omix[:16] + jnp.where(low, -rolled, rolled)).astype(BF16).astype(F32)
    lhs = jnp.concatenate([jnp.where(low, mixed, -mixed), pltpu.roll(mixed, 64, 1)], axis=0)
    lhs4 = jnp.concatenate(
        [jnp.where((lane // 16) % 4 == b, lhs, 0.0).astype(BF16) for b in range(4)], axis=0
    )
    tbm = jnp.concatenate([tb[:, 0].reshape(64, 128), tb[:, 1].reshape(64, 128)], axis=0)
    farbuf[...] = jnp.dot(lhs4, tbm, preferred_element_type=F32)

    for c in fsends:
        c.wait_recv()
    picks = []
    for b in range(4):
        picks.append(
            [jnp.minimum((nidx_s[b, k] - (p * 4 + b) + 4 + nb) % nb, 8) + b for k in range(8)]
        )
    lane2 = lax.broadcasted_iota(jnp.int32, (128, 128), 1)
    ysends = []
    for g in range(2):
        for at in range(zn):

            @pl.when(z == at)
            def _():
                for place in range(g * 4, g * 4 + 4):
                    chunk = (at + place) % zn
                    if place not in (0, reach):
                        near_arrived(chunk)

        amat = jnp.concatenate(
            [nbuf[c, (z + g * 4 + place) % zn] for c in range(2) for place in range(4)], axis=0
        )
        ysum = jnp.zeros((128, 128), F32)
        for b in range(4):
            rows_b = jnp.concatenate([fbuf[j].reshape(128, 128) for j in picks[b]], axis=1)
            ysum = jnp.where((lane2 // 4) % 4 == b, dot_nt(rows_b, amat), ysum)
        for v in range(4):
            turned = pltpu.roll(ysum[v * 32 + 16 : v * 32 + 32], 64, 1)
            ysend[g, v] = ysum[v * 32 : v * 32 + 16] + jnp.where(low, -turned, turned)
        for du in (3, 2, 1):
            xo = (xh + du // 2) % 2
            cc_ = (co + du % 2) % 2
            copy = pltpu.make_async_remote_copy(
                ysend.at[g, xo * 2 + cc_], ybuf.at[g, u], ysnd.at[g, du], yrecv.at[g, du],
                device_id=(p, inc_of(xo, z, cc_)), device_id_type=MESH,
            )
            copy.start()
            ysends.append(copy)
        ybuf[g, u] = ysend[g, u]
    for c in ysends:
        c.wait_recv()
    res_re, res_im = [], []
    for g in range(2):
        for v in (0, 2):
            even, odd = ybuf[g, v], ybuf[g, v + 1]
            res_re.append(jnp.where(low, even, pltpu.roll(odd, 64, 1)))
            res_im.append(jnp.where(low, pltpu.roll(even, 64, 1), odd))
    result = jnp.concatenate(
        [jnp.concatenate(res_re, axis=1), jnp.concatenate(res_im, axis=1)], axis=0
    )
    hi = result.astype(BF16)
    lo = (result - hi.astype(F32)).astype(BF16)
    placed = jnp.dot(jnp.concatenate([hi, lo], axis=0), pmat[...], preferred_element_type=F32)
    placed = placed[:32] + placed[32:]
    for b in range(4):
        own_b = fbuf[4 + b, u].reshape(32, 128).astype(F32)
        res = own_b * 0.5 + placed[:, b * 128 : (b + 1) * 128] + farbuf[b * 32 : (b + 1) * 32]
        out[0, :, b * 128 : (b + 1) * 128] = res[:16].astype(BF16)
        out[1, :, b * 128 : (b + 1) * 128] = res[16:].astype(BF16)
    for c in fsends + ysends:
        c.wait_send()
    for c in csends:
        c.wait_send()
    for at in range(zn):

        @pl.when(z == at)
        def _():
            for other in range(zn):
                if other != at and close(at, other):
                    near_copy(other, at).wait_send()
            relay(at).wait_send()


def solution(mesh):
    pn = mesh.shape["panel"]
    zn = mesh.shape["inc"] // 4
    nb = pn * 4
    width = 64 * zn

    def pin(x):
        return pltpu.with_memory_space_constraint(x, pltpu.HBM)

    def local(surface_field, near_block, near_index, source_basis, coupling, target_basis, far_rank):
        any_ = pl.BlockSpec(memory_space=pltpu.HBM)
        return pl.pallas_call(
            functools.partial(kernel, pn, zn),
            out_shape=jax.ShapeDtypeStruct(surface_field.shape, BF16),
            in_specs=[any_, any_, pl.BlockSpec(memory_space=pltpu.SMEM)] + [any_] * 5,
            out_specs=pl.BlockSpec(memory_space=pltpu.VMEM),
            scratch_shapes=[
                pltpu.VMEM((12, 4, 2, 16, 128), BF16),
                pltpu.VMEM((2, zn, 16, 1024), BF16),
                pltpu.VMEM((pn, 16, 128), BF16),
                pltpu.VMEM((2, 4, 16, 128), F32),
                pltpu.VMEM((2, 4, 16, 128), F32),
                pltpu.VMEM((256, 128), BF16),
                pltpu.VMEM((256, 128), F32),
                pltpu.VMEM((4, 8), jnp.int32),
                pltpu.VMEM((4, nb), jnp.int32),
                pltpu.VMEM((4, 2, 16, 128), BF16),
                pltpu.VMEM((4, 2, 16, nb * 16), BF16),
                pltpu.VMEM((4, 2, 16, 128), BF16),
                pltpu.VMEM((128, nb * 16), BF16),
                pltpu.VMEM((width, width), BF16),
                pltpu.VMEM((128, 128), F32),
                pltpu.SemaphoreType.DMA((10,)),
                pltpu.SemaphoreType.DMA((12,)),
                pltpu.SemaphoreType.DMA((12,)),
                pltpu.SemaphoreType.DMA((zn,)),
                pltpu.SemaphoreType.DMA((zn,)),
                pltpu.SemaphoreType.DMA,
                pltpu.SemaphoreType.DMA((pn,)),
                pltpu.SemaphoreType.DMA((pn,)),
                pltpu.SemaphoreType.REGULAR((8,)),
                pltpu.SemaphoreType.REGULAR((3,)),
                pltpu.SemaphoreType.DMA((2, 4)),
                pltpu.SemaphoreType.DMA((2, 4)),
                pltpu.SemaphoreType.REGULAR((zn,)),
            ],
            compiler_params=pltpu.CompilerParams(collective_id=0, has_side_effects=True, vmem_limit_bytes=8 * 1024 * 1024),
        )(
            pin(surface_field), pin(near_block.reshape(256, 128)), near_index, pin(near_index), pin(far_rank),
            pin(source_basis), pin(coupling), pin(target_basis),
        )

    return jax.shard_map(
        local,
        mesh=mesh,
        in_specs=(
            P(None, "inc", "panel"),
            P("panel", "inc", None, None, None),
            P("panel", None),
            P("panel", None, None, None),
            P("panel", None, None, None),
            P("panel", None, None, None),
            P("panel", None),
        ),
        out_specs=P(None, "inc", "panel"),
        check_vma=False,
    )
```

```python
import functools

import jax
import jax.numpy as jnp
from jax import lax
from jax.experimental import pallas as pl
from jax.experimental.pallas import tpu as pltpu
from jax.sharding import PartitionSpec as P

MESH = pl.DeviceIdType.MESH
F32 = jnp.float32
BF16 = jnp.bfloat16
NT = (((1,), (1,)), ((), ()))


def dot_nt(a, b):
    return lax.dot_general(a, b, NT, preferred_element_type=F32)


def kernel(
    pn, zn,
    field, near, nidx_s, nidx_v, frank, sbasis, coup, tbasis,
    out,
    fbuf, nbuf, cbuf, ybuf, ysend, nraw, nf32, nv, fr, vb, cp, tb, mbuf, pmat, farbuf,
    lsem, fsend, frecv, nsend, nrecv, rsend, csend, crecv, heard, met, ysnd, yrecv, ready,
):
    p = lax.axis_index("panel")
    i = lax.axis_index("inc")
    xh = i // (2 * zn)
    z = (i // 2) % zn
    co = i % 2
    u = xh * 2 + co
    nb = pn * 4

    loads = [pltpu.make_async_copy(near, nraw, lsem.at[0])]
    for b in range(4):
        loads.append(
            pltpu.make_async_copy(field.at[:, :, pl.ds(b * 128, 128)], fbuf.at[4 + b, u], lsem.at[1 + b])
        )
    loads.append(pltpu.make_async_copy(sbasis, vb, lsem.at[5]))
    loads.append(pltpu.make_async_copy(coup, cp, lsem.at[6]))
    loads.append(pltpu.make_async_copy(tbasis, tb, lsem.at[7]))
    loads.append(pltpu.make_async_copy(nidx_v, nv, lsem.at[8]))
    loads.append(pltpu.make_async_copy(frank, fr, lsem.at[9]))
    for c in loads:
        c.start()

    def inc_of(xh_, z_, co_):
        return xh_ * (2 * zn) + z_ * 2 + co_

    npeers = [(p, inc_of(xh, other, co)) for other in range(zn)]
    below = (p, inc_of(xh, (z + zn - 1) % zn, co))
    reach = zn // 2 - 1

    def close(a, b):
        return min((a - b) % zn, (b - a) % zn) <= reach

    yn = pn // 2
    first = (p // yn) * yn
    y = p % yn
    y_next = (first + (y + 1) % yn, i)
    y_prev = (first + (y + yn - 1) % yn, i)
    column = ((p + yn) % pn, i)
    fpeers = []
    for dp in range(3):
        for du in range(4):
            if dp == 1 and du == 0:
                continue
            xo = (xh + du // 2) % 2
            cc = (co + du % 2) % 2
            fpeers.append((dp, du, ((p + dp - 1 + pn) % pn, inc_of(xo, z, cc))))

    barrier = pltpu.get_barrier_semaphore()
    high = (p, inc_of((xh + 1) % 2, z, co))
    p_next, p_prev = ((p + 1) % pn, i), ((p + pn - 1) % pn, i)
    plane = [(p, inc_of(xh, z, (co + 1) % 2)), high, p_next, p_prev, y_next, y_prev, column]

    for at in range(zn - 1):

        @pl.when(z == at)
        def _():
            for other in range(at + 1, zn):
                if close(at, other):
                    pl.semaphore_signal(barrier, inc=1, device_id=npeers[other], device_id_type=MESH)

    for dev in plane:
        pl.semaphore_signal(barrier, inc=1, device_id=dev, device_id_type=MESH)

    loads[0].wait()
    nf32[...] = nraw[...].astype(F32)
    for k in range(8):
        for c in range(2):
            rows = nf32[pl.ds(k * 2 + c, 16, stride=16), :]
            nbuf[c, z, :, k * 128 : (k + 1) * 128] = rows.astype(BF16)

    earlier = 0
    for at in range(1, zn):
        earlier = earlier + jnp.where(z == at, sum(close(at, other) for other in range(at)), 0)
    pl.semaphore_wait(barrier, len(plane) + earlier)

    def near_copy(other, at):
        return pltpu.make_async_remote_copy(
            nbuf.at[:, at], nbuf.at[:, at], nsend.at[other], nrecv.at[at],
            device_id=npeers[other], device_id_type=MESH,
        )

    def near_arrived(chunk):
        pltpu.make_async_remote_copy(
            nbuf.at[:, chunk], nbuf.at[:, chunk], nsend.at[chunk], nrecv.at[chunk],
            device_id=npeers[chunk], device_id_type=MESH,
        ).wait_recv()

    def relay(at):
        chunk = (at + reach) % zn
        return pltpu.make_async_remote_copy(
            nbuf.at[:, chunk], nbuf.at[:, chunk], rsend, nrecv.at[chunk],
            device_id=below, device_id_type=MESH,
        )

    csends = [
        pltpu.make_async_remote_copy(
            cbuf.at[p], cbuf.at[p], csend.at[d], crecv.at[d], device_id=((p + d) % pn, i), device_id_type=MESH
        )
        for d in range(1, pn)
    ]
    hops = yn // 2 - 1

    def c_step(step):
        if 0 < step <= hops:
            pl.semaphore_wait(heard.at[2 * step - 2], 1)
            pl.semaphore_wait(heard.at[2 * step - 1], 1)
        if step < hops:
            pl.semaphore_signal(heard.at[2 * step], inc=1, device_id=y_next, device_id_type=MESH)
            pl.semaphore_signal(heard.at[2 * step + 1], inc=1, device_id=y_prev, device_id_type=MESH)
        elif step == hops:
            pl.semaphore_signal(heard.at[2 * hops], inc=1, device_id=column, device_id_type=MESH)
        else:
            pl.semaphore_wait(heard.at[2 * hops], 1)
            for c in csends:
                c.start()

    def run(ops, at):
        for op in ops:
            kind, step = op[0], int(op[1])
            if kind == "C":
                c_step(step)
            elif kind == "S":
                pl.semaphore_wait(ready.at[step], 1)
                near_copy(step, at).start()
            else:
                near_arrived((at + reach) % zn)
                relay(at).start()

    for at in range(1, zn):

        @pl.when(z == at)
        def _():
            lower = [other for other in range(at) if close(at, other)]
            for other in lower:
                pl.semaphore_signal(ready.at[at], inc=1, device_id=npeers[other], device_id_type=MESH)
            for other in lower:
                near_copy(other, at).start()

    pl.semaphore_signal(met.at[0], inc=1, device_id=high, device_id_type=MESH)
    c_step(0)
    fsends = []
    for dp, du, dev in fpeers:
        fsends.append(
            pltpu.make_async_remote_copy(
                fbuf.at[pl.ds(4, 4), u], fbuf.at[pl.ds((2 - dp) * 4, 4), u],
                fsend.at[dp * 4 + du], frecv.at[dp * 4 + du],
                device_id=dev, device_id_type=MESH,
            )
        )
    for c in loads[1:5]:
        c.wait()
    pl.semaphore_wait(met.at[0], 1)
    pl.semaphore_signal(met.at[1], inc=1, device_id=p_next, device_id_type=MESH)
    pl.semaphore_signal(met.at[2], inc=1, device_id=p_prev, device_id_type=MESH)

    loads[5].wait()
    lane = lax.broadcasted_iota(jnp.int32, (32, 128), 1)
    low = lax.broadcasted_iota(jnp.int32, (16, 128), 1) < 64
    sbm = jnp.concatenate([vb[:, 0].reshape(64, 128), vb[:, 1].reshape(64, 128)], axis=0)
    own = fbuf[pl.ds(4, 4), u].reshape(128, 128)
    xall = dot_nt(own, sbm)
    xsel = jnp.zeros((32, 128), F32)
    for b in range(4):
        xsel = jnp.where((lane // 16) % 4 == b, xall[b * 32 : (b + 1) * 32], xsel)
    rolled = pltpu.roll(xsel[16:], 64, 1)
    cbuf[p] = (xsel[:16] + jnp.where(low, -rolled, rolled)).astype(BF16)

    pl.semaphore_wait(met.at[1], 1)
    pl.semaphore_wait(met.at[2], 1)
    for c in fsends:
        c.start()

    early = [
        ("C1", "C2", "S1", "C3", "C4", "S2", "S3", "S5", "S6", "S7", "F0"),
        ("C1", "C2", "S2", "C3", "C4", "S3", "S4", "F0", "S6", "S7"),
        ("C1", "C2", "S3", "C3", "C4", "S4", "S5", "F0", "S7"),
        ("C1", "C2", "S4", "C3", "C4", "S5", "S6", "F0"),
        ("C1", "C2", "S5", "C3", "C4", "S6", "S7", "F0"),
        ("C1", "C2", "S6", "C3", "C4", "S7", "F0"),
        ("C1", "C2", "S7", "C3", "C4", "F0"),
        ("C1", "C2", "C3", "C4", "F0"),
    ]
    for at in range(zn):

        @pl.when(z == at)
        def _():
            run(early[at][: early[at].index("C4") + 1], at)

    for c in loads[6:]:
        c.wait()
    ids = lax.broadcasted_iota(jnp.int32, (4, nb), 1)
    is_near = nv[:, 0:1] == ids
    for k in range(1, 8):
        is_near = jnp.logical_or(is_near, nv[:, k : k + 1] == ids)
    rank = jnp.where(is_near, 0, fr[...]).astype(F32).astype(BF16)
    cols = nb * 16
    spread = (
        lax.broadcasted_iota(jnp.int32, (nb, cols), 1) // 16 == lax.broadcasted_iota(jnp.int32, (nb, cols), 0)
    ).astype(F32).astype(BF16)
    rank_cols = jnp.dot(rank, spread, preferred_element_type=F32)
    row_a = lax.broadcasted_iota(jnp.int32, (16, cols), 0).astype(F32)
    col_c = (lax.broadcasted_iota(jnp.int32, (16, cols), 1) % 16).astype(F32)
    most = jnp.maximum(row_a, col_c)
    for b in range(4):
        keep = most < jnp.broadcast_to(rank_cols[b : b + 1, :], (16, cols))
        for r in range(2):
            mbuf[r * 64 + b * 16 : r * 64 + b * 16 + 16, :] = jnp.where(
                keep, cp[b, r].astype(F32), 0.0
            ).astype(BF16)

    lanes_n = zn * 16
    width = 4 * lanes_n
    rr = lax.broadcasted_iota(jnp.int32, (width, width), 0)
    cc = lax.broadcasted_iota(jnp.int32, (width, width), 1)
    group = width // 2
    ru = (rr % group) // 64
    rz = (z + (rr // group) * 4 + (rr % 64) // 16) % zn
    rb = (rr // 4) % 4
    rt = rr % 4
    target = rb * lanes_n + ((ru // 2) * (2 * zn) + rz * 2 + ru % 2) * 4 + rt
    pmat[...] = (cc == target).astype(F32).astype(BF16)

    for at in range(zn):

        @pl.when(z == at)
        def _():
            run(early[at][early[at].index("C4") + 1 :], at)

    for c in fsends:
        c.wait_recv()
    picks = []
    for b in range(4):
        picks.append(
            [jnp.minimum((nidx_s[b, k] - (p * 4 + b) + 4 + nb) % nb, 8) + b for k in range(8)]
        )
    lane2 = lax.broadcasted_iota(jnp.int32, (128, 128), 1)
    ysends = []
    for g in range(2):
        for at in range(zn):

            @pl.when(z == at)
            def _():
                for place in range(g * 4, g * 4 + 4):
                    chunk = (at + place) % zn
                    if place not in (0, reach):
                        near_arrived(chunk)

        amat = jnp.concatenate(
            [nbuf[c, (z + g * 4 + place) % zn] for c in range(2) for place in range(4)], axis=0
        )
        ysum = jnp.zeros((128, 128), F32)
        for b in range(4):
            rows_b = jnp.concatenate([fbuf[j].reshape(128, 128) for j in picks[b]], axis=1)
            ysum = jnp.where((lane2 // 4) % 4 == b, dot_nt(rows_b, amat), ysum)
        for v in range(4):
            turned = pltpu.roll(ysum[v * 32 + 16 : v * 32 + 32], 64, 1)
            ysend[g, v] = ysum[v * 32 : v * 32 + 16] + jnp.where(low, -turned, turned)
        for du in (3, 2, 1):
            xo = (xh + du // 2) % 2
            cc_ = (co + du % 2) % 2
            copy = pltpu.make_async_remote_copy(
                ysend.at[g, xo * 2 + cc_], ybuf.at[g, u], ysnd.at[g, du], yrecv.at[g, du],
                device_id=(p, inc_of(xo, z, cc_)), device_id_type=MESH,
            )
            copy.start()
            ysends.append(copy)
        ybuf[g, u] = ysend[g, u]
    for c in csends:
        c.wait_recv()

    re_tiles, im_tiles = [], []
    for q in range(pn // 2):
        even = cbuf[2 * q].astype(F32)
        odd = cbuf[2 * q + 1].astype(F32)
        re_tiles.append(jnp.where(low, even, pltpu.roll(odd, 64, 1)).astype(BF16))
        im_tiles.append(jnp.where(low, pltpu.roll(even, 64, 1), odd).astype(BF16))
    allc = jnp.concatenate(
        [jnp.concatenate(re_tiles, axis=1), jnp.concatenate(im_tiles, axis=1)], axis=0
    )
    omix = dot_nt(allc, mbuf[...])
    rolled = pltpu.roll(omix[16:], 64, 1)
    mixed = (omix[:16] + jnp.where(low, -rolled, rolled)).astype(BF16).astype(F32)
    lhs = jnp.concatenate([jnp.where(low, mixed, -mixed), pltpu.roll(mixed, 64, 1)], axis=0)
    lhs4 = jnp.concatenate(
        [jnp.where((lane // 16) % 4 == b, lhs, 0.0).astype(BF16) for b in range(4)], axis=0
    )
    tbm = jnp.concatenate([tb[:, 0].reshape(64, 128), tb[:, 1].reshape(64, 128)], axis=0)
    farbuf[...] = jnp.dot(lhs4, tbm, preferred_element_type=F32)

    own_rows = jnp.concatenate([fbuf[4 + b, u].reshape(32, 128) for b in range(4)], axis=1)
    far_rows = jnp.concatenate([farbuf[b * 32 : (b + 1) * 32] for b in range(4)], axis=1)
    total = own_rows.astype(F32) * 0.5 + far_rows
    for g in range(2):
        for c in ysends[g * 3 : g * 3 + 3]:
            c.wait_recv()
        res_re, res_im = [], []
        for v in (0, 2):
            even, odd = ybuf[g, v], ybuf[g, v + 1]
            res_re.append(jnp.where(low, even, pltpu.roll(odd, 64, 1)))
            res_im.append(jnp.where(low, pltpu.roll(even, 64, 1), odd))
        result = jnp.concatenate(
            [jnp.concatenate(res_re, axis=1), jnp.concatenate(res_im, axis=1)], axis=0
        )
        hi = result.astype(BF16)
        lo = (result - hi.astype(F32)).astype(BF16)
        placed = jnp.dot(
            jnp.concatenate([hi, lo], axis=0), pmat[g * group : (g + 1) * group, :], preferred_element_type=F32
        )
        total = total + (placed[:32] + placed[32:])
    out[0] = total[:16].astype(BF16)
    out[1] = total[16:].astype(BF16)
    for c in fsends + ysends:
        c.wait_send()
    for c in csends:
        c.wait_send()
    for at in range(zn):

        @pl.when(z == at)
        def _():
            for other in range(zn):
                if other != at and close(at, other):
                    near_copy(other, at).wait_send()
            relay(at).wait_send()


def solution(mesh):
    pn = mesh.shape["panel"]
    zn = mesh.shape["inc"] // 4
    nb = pn * 4
    width = 64 * zn

    def pin(x):
        return pltpu.with_memory_space_constraint(x, pltpu.HBM)

    def local(surface_field, near_block, near_index, source_basis, coupling, target_basis, far_rank):
        any_ = pl.BlockSpec(memory_space=pltpu.HBM)
        return pl.pallas_call(
            functools.partial(kernel, pn, zn),
            out_shape=jax.ShapeDtypeStruct(surface_field.shape, BF16),
            in_specs=[any_, any_, pl.BlockSpec(memory_space=pltpu.SMEM)] + [any_] * 5,
            out_specs=pl.BlockSpec(memory_space=pltpu.VMEM),
            scratch_shapes=[
                pltpu.VMEM((12, 4, 2, 16, 128), BF16),
                pltpu.VMEM((2, zn, 16, 1024), BF16),
                pltpu.VMEM((pn, 16, 128), BF16),
                pltpu.VMEM((2, 4, 16, 128), F32),
                pltpu.VMEM((2, 4, 16, 128), F32),
                pltpu.VMEM((256, 128), BF16),
                pltpu.VMEM((256, 128), F32),
                pltpu.VMEM((4, 8), jnp.int32),
                pltpu.VMEM((4, nb), jnp.int32),
                pltpu.VMEM((4, 2, 16, 128), BF16),
                pltpu.VMEM((4, 2, 16, nb * 16), BF16),
                pltpu.VMEM((4, 2, 16, 128), BF16),
                pltpu.VMEM((128, nb * 16), BF16),
                pltpu.VMEM((width, width), BF16),
                pltpu.VMEM((128, 128), F32),
                pltpu.SemaphoreType.DMA((10,)),
                pltpu.SemaphoreType.DMA((12,)),
                pltpu.SemaphoreType.DMA((12,)),
                pltpu.SemaphoreType.DMA((zn,)),
                pltpu.SemaphoreType.DMA((zn,)),
                pltpu.SemaphoreType.DMA,
                pltpu.SemaphoreType.DMA((pn,)),
                pltpu.SemaphoreType.DMA((pn,)),
                pltpu.SemaphoreType.REGULAR((8,)),
                pltpu.SemaphoreType.REGULAR((3,)),
                pltpu.SemaphoreType.DMA((2, 4)),
                pltpu.SemaphoreType.DMA((2, 4)),
                pltpu.SemaphoreType.REGULAR((zn,)),
            ],
            compiler_params=pltpu.CompilerParams(collective_id=0, has_side_effects=True, vmem_limit_bytes=8 * 1024 * 1024),
        )(
            pin(surface_field), pin(near_block.reshape(256, 128)), near_index, pin(near_index), pin(far_rank),
            pin(source_basis), pin(coupling), pin(target_basis),
        )

    return jax.shard_map(
        local,
        mesh=mesh,
        in_specs=(
            P(None, "inc", "panel"),
            P("panel", "inc", None, None, None),
            P("panel", None),
            P("panel", None, None, None),
            P("panel", None, None, None),
            P("panel", None, None, None),
            P("panel", None),
        ),
        out_specs=P(None, "inc", "panel"),
        check_vma=False,
    )
```

```python
import functools

import jax
import jax.numpy as jnp
from jax import lax
from jax.experimental import pallas as pl
from jax.experimental.pallas import tpu as pltpu
from jax.sharding import PartitionSpec as P

MESH = pl.DeviceIdType.MESH
F32 = jnp.float32
BF16 = jnp.bfloat16
NT = (((1,), (1,)), ((), ()))


def dot_nt(a, b):
    return lax.dot_general(a, b, NT, preferred_element_type=F32)


def kernel(
    pn, zn,
    field, near, nidx_s, nidx_v, frank, sbasis, coup, tbasis,
    out,
    fbuf, nbuf, cbuf, ybuf, ysend, nraw, nf32, nv, fr, vb, cp, tb, mbuf, pmat, farbuf,
    lsem, fsend, frecv, nsend, nrecv, rsend, csend, crecv, heard, met, ysnd, yrecv, ready,
):
    p = lax.axis_index("panel")
    i = lax.axis_index("inc")
    xh = i // (2 * zn)
    z = (i // 2) % zn
    co = i % 2
    u = xh * 2 + co
    nb = pn * 4

    loads = [pltpu.make_async_copy(near, nraw, lsem.at[0])]
    for b in range(4):
        loads.append(
            pltpu.make_async_copy(field.at[:, :, pl.ds(b * 128, 128)], fbuf.at[4 + b, u], lsem.at[1 + b])
        )
    loads.append(pltpu.make_async_copy(sbasis, vb, lsem.at[5]))
    loads.append(pltpu.make_async_copy(coup, cp, lsem.at[6]))
    loads.append(pltpu.make_async_copy(tbasis, tb, lsem.at[7]))
    loads.append(pltpu.make_async_copy(nidx_v, nv, lsem.at[8]))
    loads.append(pltpu.make_async_copy(frank, fr, lsem.at[9]))
    for c in loads:
        c.start()

    def inc_of(xh_, z_, co_):
        return xh_ * (2 * zn) + z_ * 2 + co_

    npeers = [(p, inc_of(xh, other, co)) for other in range(zn)]
    below = (p, inc_of(xh, (z + zn - 1) % zn, co))
    reach = zn // 2 - 1

    def close(a, b):
        return min((a - b) % zn, (b - a) % zn) <= reach or {a, b} == {0, zn // 2}

    idle = (1, zn // 2 + 1)

    yn = pn // 2
    first = (p // yn) * yn
    y = p % yn
    y_next = (first + (y + 1) % yn, i)
    y_prev = (first + (y + yn - 1) % yn, i)
    column = ((p + yn) % pn, i)
    fpeers = []
    for dp in range(3):
        for du in range(4):
            if dp == 1 and du == 0:
                continue
            xo = (xh + du // 2) % 2
            cc = (co + du % 2) % 2
            fpeers.append((dp, du, ((p + dp - 1 + pn) % pn, inc_of(xo, z, cc))))

    barrier = pltpu.get_barrier_semaphore()
    high = (p, inc_of((xh + 1) % 2, z, co))
    p_next, p_prev = ((p + 1) % pn, i), ((p + pn - 1) % pn, i)
    plane = [(p, inc_of(xh, z, (co + 1) % 2)), high, p_next, p_prev, y_next, y_prev, column]

    for at in range(zn - 1):

        @pl.when(z == at)
        def _():
            for other in range(at + 1, zn):
                if close(at, other):
                    pl.semaphore_signal(barrier, inc=1, device_id=npeers[other], device_id_type=MESH)

    for dev in plane:
        pl.semaphore_signal(barrier, inc=1, device_id=dev, device_id_type=MESH)

    loads[0].wait()
    nf32[...] = nraw[...].astype(F32)
    for k in range(8):
        for c in range(2):
            rows = nf32[pl.ds(k * 2 + c, 16, stride=16), :]
            nbuf[c, z, :, k * 128 : (k + 1) * 128] = rows.astype(BF16)

    earlier = 0
    for at in range(1, zn):
        earlier = earlier + jnp.where(z == at, sum(close(at, other) for other in range(at)), 0)
    pl.semaphore_wait(barrier, len(plane) + earlier)

    def near_copy(other, at):
        return pltpu.make_async_remote_copy(
            nbuf.at[:, at], nbuf.at[:, at], nsend.at[other], nrecv.at[at],
            device_id=npeers[other], device_id_type=MESH,
        )

    def near_arrived(chunk):
        pltpu.make_async_remote_copy(
            nbuf.at[:, chunk], nbuf.at[:, chunk], nsend.at[chunk], nrecv.at[chunk],
            device_id=npeers[chunk], device_id_type=MESH,
        ).wait_recv()

    def relay(at):
        chunk = (at + reach) % zn
        return pltpu.make_async_remote_copy(
            nbuf.at[:, chunk], nbuf.at[:, chunk], rsend, nrecv.at[chunk],
            device_id=below, device_id_type=MESH,
        )

    csends = [
        pltpu.make_async_remote_copy(
            cbuf.at[p], cbuf.at[p], csend.at[d], crecv.at[d], device_id=((p + d) % pn, i), device_id_type=MESH
        )
        for d in range(1, pn)
    ]
    hops = yn // 2 - 1

    def c_step(step):
        if 0 < step <= hops:
            pl.semaphore_wait(heard.at[2 * step - 2], 1)
            pl.semaphore_wait(heard.at[2 * step - 1], 1)
        if step < hops:
            pl.semaphore_signal(heard.at[2 * step], inc=1, device_id=y_next, device_id_type=MESH)
            pl.semaphore_signal(heard.at[2 * step + 1], inc=1, device_id=y_prev, device_id_type=MESH)
        elif step == hops:
            pl.semaphore_signal(heard.at[2 * hops], inc=1, device_id=column, device_id_type=MESH)
        else:
            pl.semaphore_wait(heard.at[2 * hops], 1)
            for c in csends:
                c.start()

    def run(ops, at):
        for op in ops:
            kind, step = op[0], int(op[1])
            if kind == "C":
                c_step(step)
            elif kind == "S":
                pl.semaphore_wait(ready.at[step], 1)
                near_copy(step, at).start()
            else:
                near_arrived((at + reach) % zn)
                relay(at).start()

    for at in range(1, zn):

        @pl.when(z == at)
        def _():
            lower = [other for other in range(at) if close(at, other)]
            for other in lower:
                pl.semaphore_signal(ready.at[at], inc=1, device_id=npeers[other], device_id_type=MESH)
            for other in lower:
                near_copy(other, at).start()

    pl.semaphore_signal(met.at[0], inc=1, device_id=high, device_id_type=MESH)
    c_step(0)
    fsends = []
    for dp, du, dev in fpeers:
        fsends.append(
            pltpu.make_async_remote_copy(
                fbuf.at[pl.ds(4, 4), u], fbuf.at[pl.ds((2 - dp) * 4, 4), u],
                fsend.at[dp * 4 + du], frecv.at[dp * 4 + du],
                device_id=dev, device_id_type=MESH,
            )
        )
    for c in loads[1:5]:
        c.wait()
    pl.semaphore_wait(met.at[0], 1)
    pl.semaphore_signal(met.at[1], inc=1, device_id=p_next, device_id_type=MESH)
    pl.semaphore_signal(met.at[2], inc=1, device_id=p_prev, device_id_type=MESH)

    loads[5].wait()
    lane = lax.broadcasted_iota(jnp.int32, (32, 128), 1)
    low = lax.broadcasted_iota(jnp.int32, (16, 128), 1) < 64
    sbm = jnp.concatenate([vb[:, 0].reshape(64, 128), vb[:, 1].reshape(64, 128)], axis=0)
    own = fbuf[pl.ds(4, 4), u].reshape(128, 128)
    xall = dot_nt(own, sbm)
    xsel = jnp.zeros((32, 128), F32)
    for b in range(4):
        xsel = jnp.where((lane // 16) % 4 == b, xall[b * 32 : (b + 1) * 32], xsel)
    rolled = pltpu.roll(xsel[16:], 64, 1)
    cbuf[p] = (xsel[:16] + jnp.where(low, -rolled, rolled)).astype(BF16)

    pl.semaphore_wait(met.at[1], 1)
    pl.semaphore_wait(met.at[2], 1)
    for c in fsends:
        c.start()

    early = [
        ("C1", "C2", "S1", "C3", "C4", "S2", "S3", "S4", "S5", "S6", "S7", "F0"),
        ("C1", "C2", "S2", "C3", "C4", "S3", "S4", "S6", "S7"),
        ("C1", "C2", "S3", "C3", "C4", "S4", "S5", "F0", "S7"),
        ("C1", "C2", "S4", "C3", "C4", "S5", "S6", "F0"),
        ("C1", "C2", "S5", "C3", "C4", "S6", "S7", "F0"),
        ("C1", "C2", "S6", "C3", "C4", "S7"),
        ("C1", "C2", "S7", "C3", "C4", "F0"),
        ("C1", "C2", "C3", "C4", "F0"),
    ]
    for at in range(zn):

        @pl.when(z == at)
        def _():
            run(early[at][: early[at].index("C4") + 1], at)

    for c in loads[6:]:
        c.wait()
    ids = lax.broadcasted_iota(jnp.int32, (4, nb), 1)
    is_near = nv[:, 0:1] == ids
    for k in range(1, 8):
        is_near = jnp.logical_or(is_near, nv[:, k : k + 1] == ids)
    rank = jnp.where(is_near, 0, fr[...]).astype(F32).astype(BF16)
    cols = nb * 16
    spread = (
        lax.broadcasted_iota(jnp.int32, (nb, cols), 1) // 16 == lax.broadcasted_iota(jnp.int32, (nb, cols), 0)
    ).astype(F32).astype(BF16)
    rank_cols = jnp.dot(rank, spread, preferred_element_type=F32)
    row_a = lax.broadcasted_iota(jnp.int32, (16, cols), 0).astype(F32)
    col_c = (lax.broadcasted_iota(jnp.int32, (16, cols), 1) % 16).astype(F32)
    most = jnp.maximum(row_a, col_c)
    for b in range(4):
        keep = most < jnp.broadcast_to(rank_cols[b : b + 1, :], (16, cols))
        for r in range(2):
            mbuf[r * 64 + b * 16 : r * 64 + b * 16 + 16, :] = jnp.where(
                keep, cp[b, r].astype(F32), 0.0
            ).astype(BF16)

    lanes_n = zn * 16
    width = 4 * lanes_n
    rr = lax.broadcasted_iota(jnp.int32, (width, width), 0)
    cc = lax.broadcasted_iota(jnp.int32, (width, width), 1)
    group = width // 2
    ru = (rr % group) // 64
    rz = (z + (rr // group) * 4 + (rr % 64) // 16) % zn
    rb = (rr // 4) % 4
    rt = rr % 4
    target = rb * lanes_n + ((ru // 2) * (2 * zn) + rz * 2 + ru % 2) * 4 + rt
    pmat[...] = (cc == target).astype(F32).astype(BF16)

    for at in range(zn):

        @pl.when(z == at)
        def _():
            run(early[at][early[at].index("C4") + 1 :], at)

    for c in fsends:
        c.wait_recv()
    picks = []
    for b in range(4):
        picks.append(
            [jnp.minimum((nidx_s[b, k] - (p * 4 + b) + 4 + nb) % nb, 8) + b for k in range(8)]
        )
    lane2 = lax.broadcasted_iota(jnp.int32, (128, 128), 1)
    ysends = []
    for g in range(2):
        for at in range(zn):

            @pl.when(z == at)
            def _():
                for place in range(g * 4, g * 4 + 4):
                    chunk = (at + place) % zn
                    if place > 0 and (place != reach or at in idle):
                        near_arrived(chunk)

        amat = jnp.concatenate(
            [nbuf[c, (z + g * 4 + place) % zn] for c in range(2) for place in range(4)], axis=0
        )
        ysum = jnp.zeros((128, 128), F32)
        for b in range(4):
            rows_b = jnp.concatenate([fbuf[j].reshape(128, 128) for j in picks[b]], axis=1)
            ysum = jnp.where((lane2 // 4) % 4 == b, dot_nt(rows_b, amat), ysum)
        for v in range(4):
            turned = pltpu.roll(ysum[v * 32 + 16 : v * 32 + 32], 64, 1)
            ysend[g, v] = ysum[v * 32 : v * 32 + 16] + jnp.where(low, -turned, turned)
        for du in (3, 2, 1):
            xo = (xh + du // 2) % 2
            cc_ = (co + du % 2) % 2
            copy = pltpu.make_async_remote_copy(
                ysend.at[g, xo * 2 + cc_], ybuf.at[g, u], ysnd.at[g, du], yrecv.at[g, du],
                device_id=(p, inc_of(xo, z, cc_)), device_id_type=MESH,
            )
            copy.start()
            ysends.append(copy)
        ybuf[g, u] = ysend[g, u]
    for c in csends:
        c.wait_recv()

    re_tiles, im_tiles = [], []
    for q in range(pn // 2):
        even = cbuf[2 * q].astype(F32)
        odd = cbuf[2 * q + 1].astype(F32)
        re_tiles.append(jnp.where(low, even, pltpu.roll(odd, 64, 1)).astype(BF16))
        im_tiles.append(jnp.where(low, pltpu.roll(even, 64, 1), odd).astype(BF16))
    allc = jnp.concatenate(
        [jnp.concatenate(re_tiles, axis=1), jnp.concatenate(im_tiles, axis=1)], axis=0
    )
    omix = dot_nt(allc, mbuf[...])
    rolled = pltpu.roll(omix[16:], 64, 1)
    mixed = (omix[:16] + jnp.where(low, -rolled, rolled)).astype(BF16).astype(F32)
    lhs = jnp.concatenate([jnp.where(low, mixed, -mixed), pltpu.roll(mixed, 64, 1)], axis=0)
    lhs4 = jnp.concatenate(
        [jnp.where((lane // 16) % 4 == b, lhs, 0.0).astype(BF16) for b in range(4)], axis=0
    )
    tbm = jnp.concatenate([tb[:, 0].reshape(64, 128), tb[:, 1].reshape(64, 128)], axis=0)
    farbuf[...] = jnp.dot(lhs4, tbm, preferred_element_type=F32)

    own_rows = jnp.concatenate([fbuf[4 + b, u].reshape(32, 128) for b in range(4)], axis=1)
    far_rows = jnp.concatenate([farbuf[b * 32 : (b + 1) * 32] for b in range(4)], axis=1)
    total = own_rows.astype(F32) * 0.5 + far_rows
    for g in range(2):
        for c in ysends[g * 3 : g * 3 + 3]:
            c.wait_recv()
        res_re, res_im = [], []
        for v in (0, 2):
            even, odd = ybuf[g, v], ybuf[g, v + 1]
            res_re.append(jnp.where(low, even, pltpu.roll(odd, 64, 1)))
            res_im.append(jnp.where(low, pltpu.roll(even, 64, 1), odd))
        result = jnp.concatenate(
            [jnp.concatenate(res_re, axis=1), jnp.concatenate(res_im, axis=1)], axis=0
        )
        hi = result.astype(BF16)
        lo = (result - hi.astype(F32)).astype(BF16)
        placed = jnp.dot(
            jnp.concatenate([hi, lo], axis=0), pmat[g * group : (g + 1) * group, :], preferred_element_type=F32
        )
        total = total + (placed[:32] + placed[32:])
    out[0] = total[:16].astype(BF16)
    out[1] = total[16:].astype(BF16)
    for c in fsends + ysends:
        c.wait_send()
    for c in csends:
        c.wait_send()
    for at in range(zn):

        @pl.when(z == at)
        def _():
            for other in range(zn):
                if other != at and close(at, other):
                    near_copy(other, at).wait_send()
            if at not in idle:
                relay(at).wait_send()


def solution(mesh):
    pn = mesh.shape["panel"]
    zn = mesh.shape["inc"] // 4
    nb = pn * 4
    width = 64 * zn

    def pin(x):
        return pltpu.with_memory_space_constraint(x, pltpu.HBM)

    def local(surface_field, near_block, near_index, source_basis, coupling, target_basis, far_rank):
        any_ = pl.BlockSpec(memory_space=pltpu.HBM)
        return pl.pallas_call(
            functools.partial(kernel, pn, zn),
            out_shape=jax.ShapeDtypeStruct(surface_field.shape, BF16),
            in_specs=[any_, any_, pl.BlockSpec(memory_space=pltpu.SMEM)] + [any_] * 5,
            out_specs=pl.BlockSpec(memory_space=pltpu.VMEM),
            scratch_shapes=[
                pltpu.VMEM((12, 4, 2, 16, 128), BF16),
                pltpu.VMEM((2, zn, 16, 1024), BF16),
                pltpu.VMEM((pn, 16, 128), BF16),
                pltpu.VMEM((2, 4, 16, 128), F32),
                pltpu.VMEM((2, 4, 16, 128), F32),
                pltpu.VMEM((256, 128), BF16),
                pltpu.VMEM((256, 128), F32),
                pltpu.VMEM((4, 8), jnp.int32),
                pltpu.VMEM((4, nb), jnp.int32),
                pltpu.VMEM((4, 2, 16, 128), BF16),
                pltpu.VMEM((4, 2, 16, nb * 16), BF16),
                pltpu.VMEM((4, 2, 16, 128), BF16),
                pltpu.VMEM((128, nb * 16), BF16),
                pltpu.VMEM((width, width), BF16),
                pltpu.VMEM((128, 128), F32),
                pltpu.SemaphoreType.DMA((10,)),
                pltpu.SemaphoreType.DMA((12,)),
                pltpu.SemaphoreType.DMA((12,)),
                pltpu.SemaphoreType.DMA((zn,)),
                pltpu.SemaphoreType.DMA((zn,)),
                pltpu.SemaphoreType.DMA,
                pltpu.SemaphoreType.DMA((pn,)),
                pltpu.SemaphoreType.DMA((pn,)),
                pltpu.SemaphoreType.REGULAR((8,)),
                pltpu.SemaphoreType.REGULAR((3,)),
                pltpu.SemaphoreType.DMA((2, 4)),
                pltpu.SemaphoreType.DMA((2, 4)),
                pltpu.SemaphoreType.REGULAR((zn,)),
            ],
            compiler_params=pltpu.CompilerParams(collective_id=0, has_side_effects=True, vmem_limit_bytes=8 * 1024 * 1024),
        )(
            pin(surface_field), pin(near_block.reshape(256, 128)), near_index, pin(near_index), pin(far_rank),
            pin(source_basis), pin(coupling), pin(target_basis),
        )

    return jax.shard_map(
        local,
        mesh=mesh,
        in_specs=(
            P(None, "inc", "panel"),
            P("panel", "inc", None, None, None),
            P("panel", None),
            P("panel", None, None, None),
            P("panel", None, None, None),
            P("panel", None, None, None),
            P("panel", None),
        ),
        out_specs=P(None, "inc", "panel"),
        check_vma=False,
    )
```

```python
import functools

import jax
import jax.numpy as jnp
from jax import lax
from jax.experimental import pallas as pl
from jax.experimental.pallas import tpu as pltpu
from jax.sharding import PartitionSpec as P

MESH = pl.DeviceIdType.MESH
F32 = jnp.float32
BF16 = jnp.bfloat16
NT = (((1,), (1,)), ((), ()))


def dot_nt(a, b):
    return lax.dot_general(a, b, NT, preferred_element_type=F32)


def kernel(
    pn, zn,
    field, near, nidx_s, nidx_v, frank, sbasis, coup, tbasis,
    out,
    fbuf, nbuf, cbuf, ybuf, ysend, nraw, nf32, nv, fr, vb, cp, tb, mbuf, pmat, farbuf,
    lsem, fsend, frecv, nsend, nrecv, rsend, csend, crecv, heard, met, ysnd, yrecv, ready,
):
    p = lax.axis_index("panel")
    i = lax.axis_index("inc")
    xh = i // (2 * zn)
    z = (i // 2) % zn
    co = i % 2
    u = xh * 2 + co
    nb = pn * 4

    loads = [pltpu.make_async_copy(near, nraw, lsem.at[0])]
    for b in range(4):
        loads.append(
            pltpu.make_async_copy(field.at[:, :, pl.ds(b * 128, 128)], fbuf.at[4 + b, u], lsem.at[1 + b])
        )
    loads.append(pltpu.make_async_copy(sbasis, vb, lsem.at[5]))
    loads.append(pltpu.make_async_copy(coup, cp, lsem.at[6]))
    loads.append(pltpu.make_async_copy(tbasis, tb, lsem.at[7]))
    loads.append(pltpu.make_async_copy(nidx_v, nv, lsem.at[8]))
    loads.append(pltpu.make_async_copy(frank, fr, lsem.at[9]))
    for c in loads:
        c.start()

    def inc_of(xh_, z_, co_):
        return xh_ * (2 * zn) + z_ * 2 + co_

    npeers = [(p, inc_of(xh, other, co)) for other in range(zn)]
    below = (p, inc_of(xh, (z + zn - 1) % zn, co))
    reach = zn // 2 - 1

    def close(a, b):
        return min((a - b) % zn, (b - a) % zn) <= reach or {a, b} in ({0, 4}, {2, 6})

    idle = (1, 3, 5, 7)

    yn = pn // 2
    first = (p // yn) * yn
    y = p % yn
    y_next = (first + (y + 1) % yn, i)
    y_prev = (first + (y + yn - 1) % yn, i)
    column = ((p + yn) % pn, i)
    fpeers = []
    for dp in range(3):
        for du in range(4):
            if dp == 1 and du == 0:
                continue
            xo = (xh + du // 2) % 2
            cc = (co + du % 2) % 2
            fpeers.append((dp, du, ((p + dp - 1 + pn) % pn, inc_of(xo, z, cc))))

    barrier = pltpu.get_barrier_semaphore()
    high = (p, inc_of((xh + 1) % 2, z, co))
    p_next, p_prev = ((p + 1) % pn, i), ((p + pn - 1) % pn, i)
    plane = [(p, inc_of(xh, z, (co + 1) % 2)), high, p_next, p_prev, y_next, y_prev, column]

    for at in range(zn - 1):

        @pl.when(z == at)
        def _():
            for other in range(at + 1, zn):
                if close(at, other):
                    pl.semaphore_signal(barrier, inc=1, device_id=npeers[other], device_id_type=MESH)

    for dev in plane:
        pl.semaphore_signal(barrier, inc=1, device_id=dev, device_id_type=MESH)

    loads[0].wait()
    nf32[...] = nraw[...].astype(F32)
    for k in range(8):
        for c in range(2):
            rows = nf32[pl.ds(k * 2 + c, 16, stride=16), :]
            nbuf[c, z, :, k * 128 : (k + 1) * 128] = rows.astype(BF16)

    earlier = 0
    for at in range(1, zn):
        earlier = earlier + jnp.where(z == at, sum(close(at, other) for other in range(at)), 0)
    pl.semaphore_wait(barrier, len(plane) + earlier)

    def near_copy(other, at):
        return pltpu.make_async_remote_copy(
            nbuf.at[:, at], nbuf.at[:, at], nsend.at[other], nrecv.at[at],
            device_id=npeers[other], device_id_type=MESH,
        )

    def near_arrived(chunk):
        pltpu.make_async_remote_copy(
            nbuf.at[:, chunk], nbuf.at[:, chunk], nsend.at[chunk], nrecv.at[chunk],
            device_id=npeers[chunk], device_id_type=MESH,
        ).wait_recv()

    def relay(at):
        chunk = (at + reach) % zn
        return pltpu.make_async_remote_copy(
            nbuf.at[:, chunk], nbuf.at[:, chunk], rsend, nrecv.at[chunk],
            device_id=below, device_id_type=MESH,
        )

    csends = [
        pltpu.make_async_remote_copy(
            cbuf.at[p], cbuf.at[p], csend.at[d], crecv.at[d], device_id=((p + d) % pn, i), device_id_type=MESH
        )
        for d in range(1, pn)
    ]
    hops = yn // 2 - 1

    def c_step(step):
        if 0 < step <= hops:
            pl.semaphore_wait(heard.at[2 * step - 2], 1)
            pl.semaphore_wait(heard.at[2 * step - 1], 1)
        if step < hops:
            pl.semaphore_signal(heard.at[2 * step], inc=1, device_id=y_next, device_id_type=MESH)
            pl.semaphore_signal(heard.at[2 * step + 1], inc=1, device_id=y_prev, device_id_type=MESH)
        elif step == hops:
            pl.semaphore_signal(heard.at[2 * hops], inc=1, device_id=column, device_id_type=MESH)
        else:
            pl.semaphore_wait(heard.at[2 * hops], 1)
            for c in csends:
                c.start()

    def run(ops, at):
        for op in ops:
            kind, step = op[0], int(op[1])
            if kind == "C":
                c_step(step)
            elif kind == "S":
                pl.semaphore_wait(ready.at[step], 1)
                near_copy(step, at).start()
            else:
                near_arrived((at + reach) % zn)
                relay(at).start()

    for at in range(1, zn):

        @pl.when(z == at)
        def _():
            lower = [other for other in range(at) if close(at, other)]
            for other in lower:
                pl.semaphore_signal(ready.at[at], inc=1, device_id=npeers[other], device_id_type=MESH)
            for other in lower:
                near_copy(other, at).start()

    pl.semaphore_signal(met.at[0], inc=1, device_id=high, device_id_type=MESH)
    c_step(0)
    fsends = []
    for dp, du, dev in fpeers:
        fsends.append(
            pltpu.make_async_remote_copy(
                fbuf.at[pl.ds(4, 4), u], fbuf.at[pl.ds((2 - dp) * 4, 4), u],
                fsend.at[dp * 4 + du], frecv.at[dp * 4 + du],
                device_id=dev, device_id_type=MESH,
            )
        )
    for c in loads[1:5]:
        c.wait()
    pl.semaphore_wait(met.at[0], 1)
    pl.semaphore_signal(met.at[1], inc=1, device_id=p_next, device_id_type=MESH)
    pl.semaphore_signal(met.at[2], inc=1, device_id=p_prev, device_id_type=MESH)

    loads[5].wait()
    lane = lax.broadcasted_iota(jnp.int32, (32, 128), 1)
    low = lax.broadcasted_iota(jnp.int32, (16, 128), 1) < 64
    sbm = jnp.concatenate([vb[:, 0].reshape(64, 128), vb[:, 1].reshape(64, 128)], axis=0)
    own = fbuf[pl.ds(4, 4), u].reshape(128, 128)
    xall = dot_nt(own, sbm)
    xsel = jnp.zeros((32, 128), F32)
    for b in range(4):
        xsel = jnp.where((lane // 16) % 4 == b, xall[b * 32 : (b + 1) * 32], xsel)
    rolled = pltpu.roll(xsel[16:], 64, 1)
    cbuf[p] = (xsel[:16] + jnp.where(low, -rolled, rolled)).astype(BF16)

    pl.semaphore_wait(met.at[1], 1)
    pl.semaphore_wait(met.at[2], 1)
    for c in fsends:
        c.start()

    early = [
        ("C1", "C2", "S1", "C3", "C4", "S2", "S3", "S4", "S5", "S6", "S7", "F0"),
        ("C1", "C2", "S2", "C3", "C4", "S3", "S4", "S6", "S7"),
        ("C1", "C2", "S3", "C3", "C4", "S4", "S5", "F0", "S6", "S7"),
        ("C1", "C2", "S4", "C3", "C4", "S5", "S6"),
        ("C1", "C2", "S5", "C3", "C4", "S6", "S7", "F0"),
        ("C1", "C2", "S6", "C3", "C4", "S7"),
        ("C1", "C2", "S7", "C3", "C4", "F0"),
        ("C1", "C2", "C3", "C4"),
    ]
    for at in range(zn):

        @pl.when(z == at)
        def _():
            run(early[at][: early[at].index("C4") + 1], at)

    for c in loads[6:]:
        c.wait()
    ids = lax.broadcasted_iota(jnp.int32, (4, nb), 1)
    is_near = nv[:, 0:1] == ids
    for k in range(1, 8):
        is_near = jnp.logical_or(is_near, nv[:, k : k + 1] == ids)
    rank = jnp.where(is_near, 0, fr[...]).astype(F32).astype(BF16)
    cols = nb * 16
    spread = (
        lax.broadcasted_iota(jnp.int32, (nb, cols), 1) // 16 == lax.broadcasted_iota(jnp.int32, (nb, cols), 0)
    ).astype(F32).astype(BF16)
    rank_cols = jnp.dot(rank, spread, preferred_element_type=F32)
    row_a = lax.broadcasted_iota(jnp.int32, (16, cols), 0).astype(F32)
    col_c = (lax.broadcasted_iota(jnp.int32, (16, cols), 1) % 16).astype(F32)
    most = jnp.maximum(row_a, col_c)
    for b in range(4):
        keep = most < jnp.broadcast_to(rank_cols[b : b + 1, :], (16, cols))
        for r in range(2):
            mbuf[r * 64 + b * 16 : r * 64 + b * 16 + 16, :] = jnp.where(
                keep, cp[b, r].astype(F32), 0.0
            ).astype(BF16)

    lanes_n = zn * 16
    width = 4 * lanes_n
    rr = lax.broadcasted_iota(jnp.int32, (width, width), 0)
    cc = lax.broadcasted_iota(jnp.int32, (width, width), 1)
    group = width // 2
    ru = (rr % group) // 64
    rz = (z + (rr // group) * 4 + (rr % 64) // 16) % zn
    rb = (rr // 4) % 4
    rt = rr % 4
    target = rb * lanes_n + ((ru // 2) * (2 * zn) + rz * 2 + ru % 2) * 4 + rt
    pmat[...] = (cc == target).astype(F32).astype(BF16)

    for at in range(zn):

        @pl.when(z == at)
        def _():
            run(early[at][early[at].index("C4") + 1 :], at)

    for c in fsends:
        c.wait_recv()
    picks = []
    for b in range(4):
        picks.append(
            [jnp.minimum((nidx_s[b, k] - (p * 4 + b) + 4 + nb) % nb, 8) + b for k in range(8)]
        )
    lane2 = lax.broadcasted_iota(jnp.int32, (128, 128), 1)
    ysends = []
    for g in range(2):
        for at in range(zn):

            @pl.when(z == at)
            def _():
                for place in range(g * 4, g * 4 + 4):
                    chunk = (at + place) % zn
                    if place > 0 and (place != reach or at in idle):
                        near_arrived(chunk)

        amat = jnp.concatenate(
            [nbuf[c, (z + g * 4 + place) % zn] for c in range(2) for place in range(4)], axis=0
        )
        ysum = jnp.zeros((128, 128), F32)
        for b in range(4):
            rows_b = jnp.concatenate([fbuf[j].reshape(128, 128) for j in picks[b]], axis=1)
            ysum = jnp.where((lane2 // 4) % 4 == b, dot_nt(rows_b, amat), ysum)
        for v in range(4):
            turned = pltpu.roll(ysum[v * 32 + 16 : v * 32 + 32], 64, 1)
            ysend[g, v] = ysum[v * 32 : v * 32 + 16] + jnp.where(low, -turned, turned)
        for du in (3, 2, 1):
            xo = (xh + du // 2) % 2
            cc_ = (co + du % 2) % 2
            copy = pltpu.make_async_remote_copy(
                ysend.at[g, xo * 2 + cc_], ybuf.at[g, u], ysnd.at[g, du], yrecv.at[g, du],
                device_id=(p, inc_of(xo, z, cc_)), device_id_type=MESH,
            )
            copy.start()
            ysends.append(copy)
        ybuf[g, u] = ysend[g, u]
    for c in csends:
        c.wait_recv()

    re_tiles, im_tiles = [], []
    for q in range(pn // 2):
        even = cbuf[2 * q].astype(F32)
        odd = cbuf[2 * q + 1].astype(F32)
        re_tiles.append(jnp.where(low, even, pltpu.roll(odd, 64, 1)).astype(BF16))
        im_tiles.append(jnp.where(low, pltpu.roll(even, 64, 1), odd).astype(BF16))
    allc = jnp.concatenate(
        [jnp.concatenate(re_tiles, axis=1), jnp.concatenate(im_tiles, axis=1)], axis=0
    )
    omix = dot_nt(allc, mbuf[...])
    rolled = pltpu.roll(omix[16:], 64, 1)
    mixed = (omix[:16] + jnp.where(low, -rolled, rolled)).astype(BF16).astype(F32)
    lhs = jnp.concatenate([jnp.where(low, mixed, -mixed), pltpu.roll(mixed, 64, 1)], axis=0)
    lhs4 = jnp.concatenate(
        [jnp.where((lane // 16) % 4 == b, lhs, 0.0).astype(BF16) for b in range(4)], axis=0
    )
    tbm = jnp.concatenate([tb[:, 0].reshape(64, 128), tb[:, 1].reshape(64, 128)], axis=0)
    farbuf[...] = jnp.dot(lhs4, tbm, preferred_element_type=F32)

    own_rows = jnp.concatenate([fbuf[4 + b, u].reshape(32, 128) for b in range(4)], axis=1)
    far_rows = jnp.concatenate([farbuf[b * 32 : (b + 1) * 32] for b in range(4)], axis=1)
    total = own_rows.astype(F32) * 0.5 + far_rows
    for g in range(2):
        for c in ysends[g * 3 : g * 3 + 3]:
            c.wait_recv()
        res_re, res_im = [], []
        for v in (0, 2):
            even, odd = ybuf[g, v], ybuf[g, v + 1]
            res_re.append(jnp.where(low, even, pltpu.roll(odd, 64, 1)))
            res_im.append(jnp.where(low, pltpu.roll(even, 64, 1), odd))
        result = jnp.concatenate(
            [jnp.concatenate(res_re, axis=1), jnp.concatenate(res_im, axis=1)], axis=0
        )
        hi = result.astype(BF16)
        lo = (result - hi.astype(F32)).astype(BF16)
        placed = jnp.dot(
            jnp.concatenate([hi, lo], axis=0), pmat[g * group : (g + 1) * group, :], preferred_element_type=F32
        )
        total = total + (placed[:32] + placed[32:])
    out[0] = total[:16].astype(BF16)
    out[1] = total[16:].astype(BF16)
    for c in fsends + ysends:
        c.wait_send()
    for c in csends:
        c.wait_send()
    for at in range(zn):

        @pl.when(z == at)
        def _():
            for other in range(zn):
                if other != at and close(at, other):
                    near_copy(other, at).wait_send()
            if at not in idle:
                relay(at).wait_send()


def solution(mesh):
    pn = mesh.shape["panel"]
    zn = mesh.shape["inc"] // 4
    nb = pn * 4
    width = 64 * zn

    def pin(x):
        return pltpu.with_memory_space_constraint(x, pltpu.HBM)

    def local(surface_field, near_block, near_index, source_basis, coupling, target_basis, far_rank):
        any_ = pl.BlockSpec(memory_space=pltpu.HBM)
        return pl.pallas_call(
            functools.partial(kernel, pn, zn),
            out_shape=jax.ShapeDtypeStruct(surface_field.shape, BF16),
            in_specs=[any_, any_, pl.BlockSpec(memory_space=pltpu.SMEM)] + [any_] * 5,
            out_specs=pl.BlockSpec(memory_space=pltpu.VMEM),
            scratch_shapes=[
                pltpu.VMEM((12, 4, 2, 16, 128), BF16),
                pltpu.VMEM((2, zn, 16, 1024), BF16),
                pltpu.VMEM((pn, 16, 128), BF16),
                pltpu.VMEM((2, 4, 16, 128), F32),
                pltpu.VMEM((2, 4, 16, 128), F32),
                pltpu.VMEM((256, 128), BF16),
                pltpu.VMEM((256, 128), F32),
                pltpu.VMEM((4, 8), jnp.int32),
                pltpu.VMEM((4, nb), jnp.int32),
                pltpu.VMEM((4, 2, 16, 128), BF16),
                pltpu.VMEM((4, 2, 16, nb * 16), BF16),
                pltpu.VMEM((4, 2, 16, 128), BF16),
                pltpu.VMEM((128, nb * 16), BF16),
                pltpu.VMEM((width, width), BF16),
                pltpu.VMEM((128, 128), F32),
                pltpu.SemaphoreType.DMA((10,)),
                pltpu.SemaphoreType.DMA((12,)),
                pltpu.SemaphoreType.DMA((12,)),
                pltpu.SemaphoreType.DMA((zn,)),
                pltpu.SemaphoreType.DMA((zn,)),
                pltpu.SemaphoreType.DMA,
                pltpu.SemaphoreType.DMA((pn,)),
                pltpu.SemaphoreType.DMA((pn,)),
                pltpu.SemaphoreType.REGULAR((8,)),
                pltpu.SemaphoreType.REGULAR((3,)),
                pltpu.SemaphoreType.DMA((2, 4)),
                pltpu.SemaphoreType.DMA((2, 4)),
                pltpu.SemaphoreType.REGULAR((zn,)),
            ],
            compiler_params=pltpu.CompilerParams(collective_id=0, has_side_effects=True, vmem_limit_bytes=8 * 1024 * 1024),
        )(
            pin(surface_field), pin(near_block.reshape(256, 128)), near_index, pin(near_index), pin(far_rank),
            pin(source_basis), pin(coupling), pin(target_basis),
        )

    return jax.shard_map(
        local,
        mesh=mesh,
        in_specs=(
            P(None, "inc", "panel"),
            P("panel", "inc", None, None, None),
            P("panel", None),
            P("panel", None, None, None),
            P("panel", None, None, None),
            P("panel", None, None, None),
            P("panel", None),
        ),
        out_specs=P(None, "inc", "panel"),
        check_vma=False,
    )
```
